128 devices in a mesh: epoch: 4 (over z), patch: 32 (over x, y, core).
Axes of the slice: x: 4, y: 4, z: 4, core: 2. Of those that a mesh axis runs over, the one named last changes fastest.
Arguments:
- tile_image: bfloat16 [4096, 256, 256], P(('epoch', 'patch')), may hold values from -6 to 6
- tile_var: bfloat16 [4096, 256, 256], P(('epoch', 'patch')), may hold values from 0.25 to 4
- psf_coef: float32 [4096, 18], P(('epoch', 'patch')), may hold values from -3 to 3
- tile_patch: int32 [4096, 1], P(('epoch', 'patch')), may hold values from 0 to 31; in each aligned block of 32 rows (0 to 31, 32 to 63, ...) at most 2 rows name the same one
- tile_offset: int32 [4096, 2], P(('epoch', 'patch')), may hold values from 0 to 256
- tile_visit: int32 [4096], P(('epoch', 'patch')), may hold values from 0 to 7
- visit_scale: float32 [8], replicated, may hold values from 0.5 to 2
Outputs:
- numerator: float32 [32, 512, 512], P('patch', 'epoch')
- inv_variance: float32 [32, 512, 512], P('patch', 'epoch')
The draws below stay inside these ranges and needn't reach their ends.
Inputs may be any that keep to these rules, and one draw needn't show every extreme that they name: `tile_patch`: among the rows of one device, no patch is named more than 2 times; some patch is named exactly 2 times.
All inputs are finite; a program needn't handle non-finite values.
Results may differ from the reference program's by a relative error of at most 0.019.
Values may be sent and summed in bfloat16 or wider, within the bound.
No kernel may reach another device: no remote copies, remote signals or barrier semaphores. Data moves between devices by JAX's collectives and lax.ppermute only.
A program may use at most 256 MiB of HBM per device.

```python
import math
import jax
import jax.numpy as jnp
import numpy as np
from jax import lax

TS = 256
TILES_DEV = 32
VISITS = 8
BASES = 3
PATCH = 512
CAP = 2
TILES = 4096
N_PATCH = 32


def with_ends(array, own_key, smallest, high):
    place = [jax.random.randint(jax.random.fold_in(own_key, axis), (), 0, length) for axis, length in enumerate(array.shape)]
    longest = array.shape.index(max(array.shape))
    beside = place[:longest] + [(place[longest] + 1) % array.shape[longest]] + place[longest + 1:]
    return array.at[tuple(place)].set(smallest).at[tuple(beside)].set(high)


def level_of(rng, shape, cuts, least, top_value):
    def one(position, shards_of):
        draws = jax.random.uniform(jax.random.fold_in(jax.random.fold_in(rng, 6), position), (shards_of,), jnp.float32, least / len(cuts), top_value / len(cuts))
        return jnp.repeat(jnp.exp(draws), shape[position] // shards_of).reshape((-1,) + (1,) * (len(shape) - position - 1))

    loudness = one(*cuts[0])
    for cut in cuts[1:]:
        loudness = loudness * one(*cut)
    return loudness


def deal_out(own_key, own, number, rows, amount, top, bound, skew):
    order = jax.random.permutation(own_key, amount)
    packed, ordinary = portions_of(amount, rows * top, bound, skew, True), portions_of(amount, rows * top, bound, skew, False)
    places = jnp.arange(amount)

    def named(lengths, rotation):
        used = int((lengths > 0).sum())
        fixed = max(1, used // 4)
        shifted = fixed + (places - fixed + rotation * (used - fixed)) % max(1, amount - fixed)
        return jnp.zeros((amount,), jnp.int32).at[order[jnp.where(places < fixed, places, shifted)]].set(jnp.asarray(lengths, jnp.int32))

    lengths = jnp.where(number % 4 == 0, named(packed, number // 4), named(ordinary, number - number // 4 - 1))
    mixed = jax.random.permutation(jax.random.fold_in(own, 3), amount)
    donor, taker = mixed[0:amount // 2 * 2:2], mixed[1:amount // 2 * 2:2]
    room = jnp.minimum(lengths[donor] - 1, bound - lengths[taker]) // 2
    room = jnp.where((donor == order[0]) | (taker == order[0]) | (lengths[taker] == 0), 0, jnp.maximum(room, 0))
    shifted = jax.random.randint(jax.random.fold_in(own, 4), (amount // 2,), 0, 1 << 20) % (room + 1)
    lengths = lengths.at[donor].add(-shifted).at[taker].add(shifted)
    labels = jnp.searchsorted(jnp.cumsum(lengths), jnp.arange(rows * top), side="right").astype(jnp.int32)
    listing = labels.reshape(top, rows).T
    listing = listing[jax.random.permutation(jax.random.fold_in(own, 1), rows)]
    rotation = jax.random.randint(jax.random.fold_in(own, 2), (rows, 1), 0, top)
    return jnp.take_along_axis(listing, (jnp.arange(top)[None, :] + rotation) % top, axis=1)


def portions_of(amount, total, limit, lean, full):
    loads = [(1 << 20) // math.isqrt(standing ** lean) + 1 for standing in range(1, amount + 1)]
    largest = limit if full else min(limit, max(-(-total // amount), total * loads[0] // sum(loads)))
    least = 1 if total - largest >= amount - 1 else 0
    given, spare = [largest] + [least] * (amount - 1), total - largest - least * (amount - 1)
    while spare > 0:
        movable = [i for i in range(1, amount) if given[i] < largest] or [i for i in range(1, amount) if given[i] < limit]
        mass, remaining = sum([loads[i] for i in movable]), spare
        for i in movable:
            extra = min(limit - given[i], max(1, remaining * loads[i] // mass), spare)
            given[i] = given[i] + extra
            spare = spare - extra
    return np.array(given)


def bell_draw(stream_key, dims, deviation, reach, cuts=(), dtype=jnp.bfloat16):
    array = jax.random.normal(stream_key, dims, jnp.float32) * deviation
    if len(cuts) > 0:
        array = level_of(stream_key, dims, cuts, -0.22, 0.18) * array
    return jnp.clip(array, min=-reach, max=reach).astype(dtype)


def setup_inputs(seed: int = 0) -> dict:
    streams_of = jax.random.split(jax.random.key(seed), 8)
    tile_image = bell_draw(streams_of[0], (TILES, TS, TS), 1.0, 6.0, ((0, 128),))
    tile_var = jnp.clip(jnp.exp(math.log(4.0) - 2.7725887 * jax.random.uniform(streams_of[1], (TILES, TS, TS), jnp.float32) ** level_of(streams_of[1], (TILES, TS, TS), ((0, 128),), -0.2, 0.2)), 0.25, 4.0).astype(jnp.bfloat16)
    psf_coef = bell_draw(streams_of[2], (TILES, 6 * BASES), 0.5, 3.0, ((0, 128),), jnp.float32)
    tile_patch_keys = jax.random.split(jax.random.fold_in(streams_of[3], 1), TILES // TILES_DEV)
    tile_patch_turns = jax.random.permutation(jax.random.fold_in(streams_of[3], 3), TILES // TILES_DEV)
    tile_patch = jax.vmap(lambda own, number: deal_out(jax.random.fold_in(streams_of[3], 2), own, number, TILES_DEV, N_PATCH, 1, CAP, 2))(tile_patch_keys, tile_patch_turns).reshape((TILES, 1))
    tile_offset = with_ends(jax.random.randint(streams_of[4], (TILES, 2), 0, TS + 1), jax.random.fold_in(streams_of[4], 1), 0, TS).astype(jnp.int32)
    tile_visit = with_ends(jax.random.randint(streams_of[5], (TILES,), 0, VISITS), jax.random.fold_in(streams_of[5], 1), 0, VISITS - 1).astype(jnp.int32)
    visit_scale = jnp.clip(jnp.exp(jax.random.uniform(streams_of[6], (VISITS,), jnp.float32, math.log(0.5), math.log(2.0))), 0.5, 2.0)
    return dict(tile_image=tile_image, tile_var=tile_var, psf_coef=psf_coef, tile_patch=tile_patch, tile_offset=tile_offset, tile_visit=tile_visit, visit_scale=visit_scale)


sigmas = (1.0, 2.0, 3.5)
kernel_reach = 7


def kernels(tile_side):
    positions = jnp.arange(tile_side)
    distance = (positions[:, None] - positions[None, :]).astype(jnp.float32)
    tap_offsets = jnp.arange(-kernel_reach, kernel_reach + 1).astype(jnp.float32)
    tables = []
    for sigma in sigmas:
        profile = jnp.where(jnp.abs(distance) <= kernel_reach, jnp.exp(-distance * distance / (2.0 * sigma * sigma)), 0.0)
        summed = jnp.sum(jnp.exp(-tap_offsets * tap_offsets / (2.0 * sigma * sigma)))
        tables.append(profile / summed)
    return jnp.stack(tables).astype(jnp.bfloat16)


def poly_terms(tile_side):
    coordinate = (2.0 * jnp.arange(tile_side).astype(jnp.float32) + 1.0) / tile_side - 1.0
    row_coord = jnp.broadcast_to(coordinate[:, None], (tile_side, tile_side))
    column_coord = jnp.broadcast_to(coordinate[None, :], (tile_side, tile_side))
    return jnp.stack([jnp.ones_like(row_coord), row_coord, column_coord, row_coord * row_coord, row_coord * column_coord, column_coord * column_coord])


def match_tiles(image_tiles, variance, coefficients, visit_gain, present):
    tile_side = image_tiles.shape[-1]
    kernel = kernels(tile_side)
    terms = poly_terms(tile_side)
    factors = coefficients.reshape(-1, 3, 6).astype(jnp.float32)
    matched = jnp.zeros(image_tiles.shape, jnp.float32)
    for basis in range(3):
        row_pass = jnp.einsum('nij,kj->nik', image_tiles, kernel[basis], preferred_element_type=jnp.float32).astype(jnp.bfloat16)
        blurred = jnp.einsum('li,nik->nlk', kernel[basis], row_pass, preferred_element_type=jnp.float32)
        spatial = jnp.einsum('nj,jlk->nlk', factors[:, basis], terms, precision=lax.Precision.HIGHEST)
        matched = matched + spatial * blurred
    weights = present[:, None, None] / (variance.astype(jnp.float32) + (1.0 - present)[:, None, None])
    weighted = visit_gain[:, None, None] * weights * matched
    return jnp.stack([weighted, weights], axis=1).astype(jnp.bfloat16)


def reference(tile_image, tile_var, psf_coef, tile_patch, tile_offset, tile_visit, visit_scale):
    tile_count = tile_image.shape[0]
    block_count = tile_count // TILES_DEV
    zero_index = jnp.zeros((), jnp.int32)

    def one_block(running, block_index):
        start = (block_index * TILES_DEV).astype(jnp.int32)
        images = lax.dynamic_slice_in_dim(tile_image, start, TILES_DEV, 0)
        variance = lax.dynamic_slice_in_dim(tile_var, start, TILES_DEV, 0)
        coefficients = lax.dynamic_slice_in_dim(psf_coef, start, TILES_DEV, 0)
        targets = lax.dynamic_slice_in_dim(tile_patch, start, TILES_DEV, 0)[:, 0].astype(jnp.int32)
        offsets = lax.dynamic_slice_in_dim(tile_offset, start, TILES_DEV, 0).astype(jnp.int32)
        visits = lax.dynamic_slice_in_dim(tile_visit, start, TILES_DEV, 0)
        visit_gain = visit_scale[visits]
        present = jnp.ones((TILES_DEV,), jnp.float32)
        tiles = match_tiles(images, variance, coefficients, visit_gain, present)

        def add_tile(member, summed):
            corner = (zero_index, targets[member], offsets[member, 0], offsets[member, 1])
            region = lax.dynamic_slice(summed, corner, (2, 1, TS, TS))
            region = region + tiles[member][:, None].astype(jnp.float32)
            return lax.dynamic_update_slice(summed, region, corner)

        return lax.fori_loop(0, TILES_DEV, add_tile, running), None

    initial = jnp.zeros((2, N_PATCH, PATCH, PATCH), jnp.float32)
    summed, unused = lax.scan(one_block, initial, jnp.arange(block_count))
    return summed[0], summed[1]
```

```python
import functools

import jax
import jax.numpy as jnp
import numpy as np
from jax import lax
from jax.experimental import pallas as pl
from jax.experimental.pallas import tpu as pltpu
from jax.sharding import PartitionSpec as P

SIGMAS = (1.0, 2.0, 3.5)
REACH = 7
GROUP = 4
UNROLL = 4


def blur_kernels(side):
    place = np.arange(side)
    distance = (place[:, None] - place[None, :]).astype(np.float32)
    taps = np.arange(-REACH, REACH + 1).astype(np.float32)
    tables = []
    for sigma in SIGMAS:
        scale = np.float32(2.0 * sigma * sigma)
        profile = np.where(np.abs(distance) <= REACH, np.exp(-distance * distance / scale), np.float32(0.0))
        tables.append(profile / np.sum(np.exp(-taps * taps / scale), dtype=np.float32))
    return np.concatenate(tables, axis=1).astype(jnp.bfloat16)


def fold_rows(side, rows_ref):
    @pl.when(pl.program_id(0) == 0)
    def _():
        s = lax.broadcasted_iota(jnp.int32, (side, side), 0)
        rows_ref[...] = ((s >> 2) & 1) * (side // 2) + 4 * (s >> 3) + (s & 3)


def fold(tile, off_r, off_c, rows_ref):
    side = tile.shape[0]
    lanes = lax.broadcasted_iota(jnp.int32, (side, side), 1)
    pick = ((lanes + off_r) & (side - 1)) == rows_ref[...]
    turn = jnp.where(pick, 1.0, 0.0).astype(jnp.bfloat16)
    placed = jnp.dot(turn, tile, preferred_element_type=jnp.float32)
    return pltpu.roll(placed, off_c & (side - 1), 1)


def weight_body(off_ref, var_ref, out_ref, rows_ref):
    parts = out_ref.shape[0]
    side = var_ref.shape[-1]
    fold_rows(side, rows_ref)
    for t in range(GROUP):
        tile = pl.program_id(0) * GROUP + t
        weight = (1.0 / var_ref[t].astype(jnp.float32)).astype(jnp.bfloat16)
        placed = fold(weight, off_ref[0, tile], off_ref[1, tile], rows_ref)
        out_ref[:, t] = placed.reshape(parts, side // parts, side).astype(jnp.bfloat16)


def value_body(off_ref, visit_ref, scale_ref, coef_ref, kernel_ref, image_ref, var_ref, out_ref, rows_ref, blur_ref, tile_ref):
    parts = out_ref.shape[0]
    side = var_ref.shape[-1]
    fold_rows(side, rows_ref)
    chunk = 32
    x = (2.0 * lax.broadcasted_iota(jnp.int32, (chunk, side), 1).astype(jnp.float32) + 1.0) / side - 1.0
    rows = lax.broadcasted_iota(jnp.int32, (chunk, side), 0)
    for t in range(GROUP):
        tile = pl.program_id(0) * GROUP + t
        gain = scale_ref[visit_ref[tile]]
        row_pass = jnp.dot(image_ref[t], kernel_ref[...], preferred_element_type=jnp.float32).astype(jnp.bfloat16)
        for b in range(3):
            cols = slice(b * side, (b + 1) * side)
            blur_ref[b] = jnp.dot(kernel_ref[:, cols], row_pass[:, cols], preferred_element_type=jnp.float32)
        for c in range(side // chunk):
            band = slice(c * chunk, (c + 1) * chunk)
            y = (2.0 * (rows + c * chunk).astype(jnp.float32) + 1.0) / side - 1.0
            matched = None
            for b in range(3):
                k = [coef_ref[6 * b + j, tile] for j in range(6)]
                spatial = (k[0] + y * (k[1] + k[3] * y)) + x * ((k[2] + k[4] * y) + k[5] * x)
                term = spatial * blur_ref[b, band]
                matched = term if matched is None else matched + term
            weight = 1.0 / var_ref[t, band].astype(jnp.float32)
            tile_ref[band] = (gain * weight * matched).astype(jnp.bfloat16)
        placed = fold(tile_ref[...], off_ref[0, tile], off_ref[1, tile], rows_ref)
        out_ref[:, t] = placed.reshape(parts, side // parts, side).astype(jnp.bfloat16)


def sum_body(start_ref, order_ref, part_ref, data_ref, *refs):
    out_ref = refs[-1]
    patches = start_ref.shape[0] - 1
    height, side = data_ref.shape[-2:]
    s = lax.broadcasted_iota(jnp.int32, (height, side), 0)
    row = (s >> 2) * (side // 2) + 4 * part_ref[0] + (s & 3)
    lane = lax.broadcasted_iota(jnp.int32, (height, side), 1)
    first = lax.broadcasted_iota(jnp.int32, (height, 2 * side), 0) < height // 2
    zero = jnp.zeros((height, side), jnp.float32)

    def one_patch(p, unused):
        begin, end = start_ref[p], start_ref[p + 1]

        def some_tiles(step, sums):
            sums = list(sums)
            for u in range(UNROLL):
                k = begin + step * UNROLL + u
                word = order_ref[jnp.minimum(k, end - 1)]
                there = jnp.where(k < end, 1.0, 0.0)
                tile, off_r, off_c = word & 1023, (word >> 10) & 511, word >> 19
                value = data_ref[tile].astype(jnp.float32) * there
                left = jnp.where(lane >= off_c, value, 0.0)
                right = value - left
                upper = row >= off_r
                sums[0] += jnp.where(upper, left, 0.0)
                sums[1] += jnp.where(upper, right, 0.0)
                sums[2] += jnp.where(upper, 0.0, left)
                sums[3] += jnp.where(upper, 0.0, right)
            return tuple(sums)

        sums = lax.fori_loop(0, (end - begin + UNROLL - 1) // UNROLL, some_tiles, (zero,) * 4)
        for half in range(2):
            mine = jnp.concatenate([sums[2 * half], sums[2 * half + 1]], axis=1)
            if len(refs) == 1:
                out_ref[half, p] = mine
            else:
                other = refs[0][half, p]
                swap = height // 2
                out_ref[2 * half, p] = jnp.where(first, mine, pltpu.roll(other, swap, 0)).astype(jnp.bfloat16)
                out_ref[2 * half + 1, p] = jnp.where(first, pltpu.roll(mine, swap, 0), other).astype(jnp.bfloat16)
        return unused

    lax.fori_loop(0, patches, one_patch, 0)


def final_body(got_ref, value_ref, weight_ref):
    epochs, parts, height, width = got_ref.shape
    swap = height // 2
    first = lax.broadcasted_iota(jnp.int32, (height, width), 0) < swap
    for pair in range(parts // 2):
        both = []
        for part in (2 * pair, 2 * pair + 1):
            total = got_ref[0, part].astype(jnp.float32)
            for e in range(1, epochs):
                total = total + got_ref[e, part].astype(jnp.float32)
            both.append(total)
        rows = slice(pair * height, (pair + 1) * height)
        value_ref[0, rows] = jnp.where(first, both[0], pltpu.roll(both[1], swap, 0))
        weight_ref[0, rows] = jnp.where(first, pltpu.roll(both[0], swap, 0), both[1])


def shards(tile_image, tile_var, psf_coef, tile_patch, tile_offset, tile_visit, visit_scale):
    count, side = tile_image.shape[:2]
    parts = lax.axis_size("patch")
    epochs = lax.axis_size("epoch")
    height = side // parts
    me = lax.axis_index("patch")
    table = jnp.asarray(blur_kernels(side))

    brief = (tile_patch + (tile_offset[:, :1] << 5) + (tile_offset[:, 1:] << 14))[:, 0]
    known = lax.all_to_all(jnp.broadcast_to(brief[None], (parts, count)), "patch", split_axis=0, concat_axis=0, tiled=True)
    known = known.reshape(-1)
    place = jnp.arange(parts * count, dtype=jnp.int32)
    target, word = known & 31, (known >> 5 << 10) + place
    ahead = (target[None, :] < target[:, None]) | ((target[None, :] == target[:, None]) & (place[None, :] < place[:, None]))
    rank = jnp.sum(ahead.astype(jnp.int32), axis=1)
    order = jnp.sum(jnp.where(rank[None, :] == place[:, None], word[None, :], 0), axis=1)
    start = jnp.sum((target[None, :] < jnp.arange(parts + 1, dtype=jnp.int32)[:, None]).astype(jnp.int32), axis=1)

    smem = pl.BlockSpec(memory_space=pltpu.SMEM)
    whole = lambda shape: pl.BlockSpec(shape, lambda g: (0,) * len(shape))
    tiles = pl.BlockSpec((GROUP, side, side), lambda g: (g, 0, 0))
    sent = pl.BlockSpec((parts, GROUP, height, side), lambda g: (0, g, 0, 0))
    sent_shape = jax.ShapeDtypeStruct((parts, count, height, side), jnp.bfloat16)
    pixels = count * side * side
    weights = pl.pallas_call(
        weight_body,
        grid=(count // GROUP,),
        in_specs=[smem, tiles],
        out_specs=sent,
        out_shape=sent_shape,
        scratch_shapes=[pltpu.VMEM((side, side), jnp.int32)],
        cost_estimate=pl.CostEstimate(flops=2 * pixels * side, bytes_accessed=4 * pixels, transcendentals=0),
        name="weights",
    )(tile_offset.T, tile_var)
    tile_image, weights = lax.optimization_barrier((tile_image, weights))
    values = pl.pallas_call(
        value_body,
        grid=(count // GROUP,),
        in_specs=[smem, smem, smem, smem, whole((side, 3 * side)), tiles, tiles],
        out_specs=sent,
        out_shape=sent_shape,
        scratch_shapes=[pltpu.VMEM((side, side), jnp.int32), pltpu.VMEM((3, side, side), jnp.float32), pltpu.VMEM((side, side), jnp.bfloat16)],
        cost_estimate=pl.CostEstimate(flops=14 * pixels * side, bytes_accessed=6 * pixels, transcendentals=0),
        compiler_params=pltpu.CompilerParams(vmem_limit_bytes=40 << 20),
        name="values",
    )(tile_offset.T, tile_visit, visit_scale, psf_coef.T, table, tile_image, tile_var)

    vmem = pl.BlockSpec(memory_space=pltpu.VMEM)

    def by_patch(sent_rows, name, *other):
        got = lax.all_to_all(sent_rows, "patch", split_axis=0, concat_axis=0, tiled=True)
        got = got.reshape(parts * count, height, side)
        out = (4, jnp.bfloat16) if other else (2, jnp.float32)
        return pl.pallas_call(
            sum_body,
            in_specs=[smem, smem, smem, vmem] + [vmem] * len(other),
            out_specs=vmem,
            out_shape=jax.ShapeDtypeStruct((out[0], parts, height, 2 * side), out[1]),
            cost_estimate=pl.CostEstimate(flops=10 * pixels, bytes_accessed=3 * pixels, transcendentals=0),
            compiler_params=pltpu.CompilerParams(vmem_limit_bytes=32 << 20),
            name=name,
        )(start, order, me[None], got, *other)

    weight_sums = by_patch(weights, "weight_sums")
    sums = by_patch(values, "value_sums", weight_sums)
    sums = sums.reshape(epochs * parts, height, 2 * side)
    got = lax.all_to_all(sums, ("epoch", "patch"), split_axis=0, concat_axis=0, tiled=True)
    quarter = jax.ShapeDtypeStruct((1, 4 * parts, 2 * side), jnp.float32)
    return pl.pallas_call(
        final_body,
        in_specs=[vmem],
        out_specs=(vmem, vmem),
        out_shape=(quarter, quarter),
        name="final",
    )(got.reshape(epochs, parts, height, 2 * side))


def solution(mesh):
    placed = (
        P(("epoch", "patch"), None, None),
        P(("epoch", "patch"), None, None),
        P(("epoch", "patch"), None),
        P(("epoch", "patch"), None),
        P(("epoch", "patch"), None),
        P(("epoch", "patch")),
        P(),
    )
    return jax.shard_map(
        shards,
        mesh=mesh,
        in_specs=placed,
        out_specs=(P("patch", "epoch", None), P("patch", "epoch", None)),
        check_vma=False,
    )
```

```python
import jax
import jax.numpy as jnp
import numpy as np
from jax import lax
from jax.experimental import pallas as pl
from jax.experimental.pallas import tpu as pltpu
from jax.sharding import PartitionSpec as P

SIGMAS = (1.0, 2.0, 3.5)
REACH = 7
GROUP = 4


def blur_kernels(side):
    place = np.arange(side)
    distance = (place[:, None] - place[None, :]).astype(np.float32)
    taps = np.arange(-REACH, REACH + 1).astype(np.float32)
    tables = []
    for sigma in SIGMAS:
        scale = np.float32(2.0 * sigma * sigma)
        profile = np.where(np.abs(distance) <= REACH, np.exp(-distance * distance / scale), np.float32(0.0))
        tables.append(profile / np.sum(np.exp(-taps * taps / scale), dtype=np.float32))
    return np.concatenate(tables, axis=1).astype(jnp.bfloat16)


def keep_turned(value, off_c, wide_ref, first_row):
    rows, side = value.shape
    turned = pltpu.roll(value, off_c & (side - 1), 1)
    for h in range(2):
        lanes = turned[:, h * (side // 2) : (h + 1) * (side // 2)]
        wide_ref[h, first_row : first_row + rows] = lanes
        wide_ref[h, first_row + side : first_row + side + rows] = lanes


def table_of_tiles(patch_ref, off_ref, shape):
    lane = lax.broadcasted_iota(jnp.int32, shape, 1)
    row = lax.broadcasted_iota(jnp.int32, shape, 0)
    known = jnp.zeros(shape, jnp.int32)
    for t in range(patch_ref.shape[1]):
        mine = jnp.where(row == 0, patch_ref[0, t], jnp.where(row == 1, off_ref[0, t], off_ref[1, t]))
        known = jnp.where((lane == t) & (row < 3), mine, known)
    return known.astype(jnp.float32).astype(jnp.bfloat16)


def weight_body(patch_ref, off_ref, var_ref, out_ref, wide_ref):
    parts, group, height, side = out_ref.shape
    step = pl.program_id(0)
    half, swap = side // 2, height // 2
    chunk = 32

    @pl.when(step < pl.num_programs(0) - 1)
    def _():
        first = lax.broadcasted_iota(jnp.int32, (height, half), 0) < swap
        for t in range(group):
            tile = step * group + t
            off_r, off_c = off_ref[0, tile], off_ref[1, tile]
            for c in range(side // chunk):
                weight = 1.0 / var_ref[t, c * chunk : (c + 1) * chunk].astype(jnp.float32)
                keep_turned(weight, off_c, wide_ref.at[t], c * chunk)
            for part in range(parts):
                begins = [(4 * part - off_r) & (side - 1), (half + 4 * part - swap - off_r) & (side - 1)]
                for h in range(2):
                    rows = [wide_ref[t, h, pl.ds(begin, height)] for begin in begins]
                    out_ref[part, t, :, h * half : (h + 1) * half] = jnp.where(first, *rows).astype(jnp.bfloat16)

    @pl.when(step == pl.num_programs(0) - 1)
    def _():
        known = table_of_tiles(patch_ref, off_ref, (height, side))
        for part in range(parts):
            out_ref[part, 0] = known


def value_body(me_ref, patch_ref, off_ref, visit_ref, scale_ref, coef_ref, kernel_ref, image_ref, var_ref, *refs):
    outs, (blur_ref, wide_ref) = refs[:8], refs[8:]
    group, height, side = outs[0].shape
    step = pl.program_id(0)
    half, band = side // 2, height // 2
    chunk = 32

    @pl.when(step < pl.num_programs(0) - 1)
    def _():
        lane = lax.broadcasted_iota(jnp.int32, (chunk, half), 1)
        row = lax.broadcasted_iota(jnp.int32, (chunk, half), 0)
        xs = [(2.0 * (lane + h * half).astype(jnp.float32) + 1.0) / side - 1.0 for h in range(2)]
        for t in range(group):
            tile = step * group + t
            off_r, off_c = off_ref[0, tile], off_ref[1, tile]
            gain = scale_ref[visit_ref[tile]]
            k = [[coef_ref[6 * b + j, tile] for j in range(6)] for b in range(3)]
            square = [[k[b][5] * x for x in xs] for b in range(3)]
            row_pass = jnp.dot(image_ref[t], kernel_ref[...], preferred_element_type=jnp.float32).astype(jnp.bfloat16)
            for b in range(3):
                cols = slice(b * side, (b + 1) * side)
                blur_ref[t, b] = jnp.dot(kernel_ref[:, cols], row_pass[:, cols], preferred_element_type=jnp.float32)
            for c in range(side // chunk):
                rows = slice(c * chunk, (c + 1) * chunk)
                y = (2.0 * (row + c * chunk).astype(jnp.float32) + 1.0) / side - 1.0
                level = [k[b][0] + y * (k[b][1] + k[b][3] * y) for b in range(3)]
                slope = [k[b][2] + k[b][4] * y for b in range(3)]
                both = []
                for h in range(2):
                    cols = slice(h * half, (h + 1) * half)
                    matched = None
                    for b in range(3):
                        spatial = level[b] + xs[h] * (slope[b] + square[b][h])
                        term = spatial * blur_ref[t, b, rows, cols]
                        matched = term if matched is None else matched + term
                    both.append(gain * (1.0 / var_ref[t, rows, cols].astype(jnp.float32)) * matched)
                keep_turned(jnp.concatenate(both, axis=1), off_c, wide_ref.at[t], c * chunk)
            for m in range(8):
                member = (((me_ref[0] + (m & 3)) & 3) << 1) + (me_ref[1] ^ (m >> 2))
                for part in range(2):
                    begin = (part * half + (member << 4) - off_r) & (side - 1)
                    for h in range(2):
                        rows = wide_ref[t, h, pl.ds(begin, band)]
                        outs[m][t, part * band : (part + 1) * band, h * half : (h + 1) * half] = rows.astype(jnp.bfloat16)

    @pl.when(step == pl.num_programs(0) - 1)
    def _():
        known = table_of_tiles(patch_ref, off_ref, (height, side))
        for m in range(8):
            outs[m][0] = known


def sum_tiles(start_ref, order_ref, p, data_ref, row, lane, unroll):
    begin, end = start_ref[p], start_ref[p + 1]
    zero = jnp.zeros(row.shape, jnp.float32)

    def some_tiles(step, sums):
        sums = list(sums)
        for u in range(unroll):
            n = begin + step * unroll + u
            word = order_ref[jnp.minimum(n, end - 1)]
            there = jnp.where(n < end, 1.0, 0.0)
            tile, off_r, off_c = word & 2047, (word >> 11) & 511, word >> 20
            value = data_ref[tile].astype(jnp.float32) * there
            left = jnp.where(lane >= off_c, value, 0.0)
            right = value - left
            upper = row >= off_r
            sums[0] += jnp.where(upper, left, 0.0)
            sums[1] += jnp.where(upper, right, 0.0)
            sums[2] += jnp.where(upper, 0.0, left)
            sums[3] += jnp.where(upper, 0.0, right)
        return tuple(sums)

    return lax.fori_loop(0, (end - begin + unroll - 1) // unroll, some_tiles, (zero,) * 4)


def weight_sum_body(start_ref, order_ref, me_ref, data_ref, out_ref):
    height, side = data_ref.shape[-2:]
    s = lax.broadcasted_iota(jnp.int32, (height, side), 0)
    row = (s >> 2) * (side // 2) + 4 * me_ref[2] + (s & 3)
    lane = lax.broadcasted_iota(jnp.int32, (height, side), 1)
    swap = height // 2
    first = s < swap

    def one_patch(p, unused):
        sums = sum_tiles(start_ref, order_ref, p, data_ref, row, lane, 4)
        for half in range(2):
            left, right = sums[2 * half], sums[2 * half + 1]
            out_ref[2 * half, p] = jnp.where(first, left, pltpu.roll(right, swap, 0)).astype(jnp.bfloat16)
            out_ref[2 * half + 1, p] = jnp.where(first, pltpu.roll(left, swap, 0), right).astype(jnp.bfloat16)
        return unused

    lax.fori_loop(0, out_ref.shape[1], one_patch, 0)


def value_sum_body(start_ref, order_ref, me_ref, weight_ref, *refs):
    got, out_ref, (data_ref, sems) = refs[:8], refs[8], refs[9:]
    slots, height, side = got[0].shape
    copies = [pltpu.make_async_copy(got[m], data_ref.at[pl.ds(m * slots, slots)], sems.at[m]) for m in range(8)]
    for copy in copies:
        copy.start()
    s = lax.broadcasted_iota(jnp.int32, (height, side), 0)
    band = height // 2
    row = (s >> 4) * (side // 2) + (((me_ref[0] << 1) + me_ref[1]) << 4) + (s & 15)
    lane = lax.broadcasted_iota(jnp.int32, (height, side), 1)
    for copy in copies:
        copy.wait()

    def one_patch(p, unused):
        sums = sum_tiles(start_ref, order_ref, p, data_ref, row, lane, 2)
        for quarter in range(4):
            rows = slice((quarter & 1) * band, ((quarter & 1) + 1) * band)
            for h in range(2):
                part = sums[2 * (quarter >> 1) + h][rows]
                out_ref[quarter, p, h * band : (h + 1) * band] = part.astype(jnp.bfloat16)
            out_ref[quarter, p, height:] = weight_ref[quarter, p]
        return unused

    lax.fori_loop(0, out_ref.shape[1], one_patch, 0)


def final_body(got_ref, value_ref, weight_ref):
    epochs, parts, height, side = got_ref.shape
    band = 16
    for z in range(epochs):
        for core in range(2):
            rows = slice((2 * z + core) * band, (2 * z + core + 1) * band)
            for h in range(2):
                total = jnp.zeros((band, side), jnp.float32)
                for chip in range(parts // 2):
                    total += got_ref[z, 2 * chip + core, h * band : (h + 1) * band].astype(jnp.float32)
                value_ref[0, rows, h * side : (h + 1) * side] = total
    swap = 4
    first = lax.broadcasted_iota(jnp.int32, (8, side), 0) < swap
    for pair in range(parts // 2):
        both = []
        for part in (2 * pair, 2 * pair + 1):
            total = got_ref[0, part, 2 * band :].astype(jnp.float32)
            for e in range(1, epochs):
                total += got_ref[e, part, 2 * band :].astype(jnp.float32)
            both.append(total)
        rows = slice(pair * 8, (pair + 1) * 8)
        weight_ref[0, rows, :side] = jnp.where(first, both[0], pltpu.roll(both[1], swap, 0))
        weight_ref[0, rows, side:] = jnp.where(first, pltpu.roll(both[0], swap, 0), both[1])


def by_patch(known, slots, patches):
    known = known.astype(jnp.float32).astype(jnp.int32)
    sources, _, count = known.shape
    where = lax.broadcasted_iota(jnp.int32, (sources, count), 0) * slots + lax.broadcasted_iota(jnp.int32, (sources, count), 1)
    word = (where + (known[:, 1] << 11) + (known[:, 2] << 20)).reshape(-1)
    target = known[:, 0].reshape(-1)
    place = jnp.arange(sources * count, dtype=jnp.int32)
    ahead = (target[None, :] < target[:, None]) | ((target[None, :] == target[:, None]) & (place[None, :] < place[:, None]))
    rank = jnp.sum(ahead.astype(jnp.int32), axis=1)
    order = jnp.sum(jnp.where(rank[None, :] == place[:, None], word[None, :], 0), axis=1)
    start = jnp.sum((target[None, :] < jnp.arange(patches + 1, dtype=jnp.int32)[:, None]).astype(jnp.int32), axis=1)
    return start, order


def shards(tile_image, tile_var, psf_coef, tile_patch, tile_offset, tile_visit, visit_scale):
    count, side = tile_image.shape[:2]
    parts = lax.axis_size("patch")
    epochs = lax.axis_size("epoch")
    height = side // parts
    slots = count + 1
    z, j = lax.axis_index("epoch"), lax.axis_index("patch")
    me = jnp.stack([z, j & 1, j]).astype(jnp.int32)
    table = jnp.asarray(blur_kernels(side))

    smem = pl.BlockSpec(memory_space=pltpu.SMEM)
    vmem = pl.BlockSpec(memory_space=pltpu.VMEM)
    steps = count // GROUP
    tiles = pl.BlockSpec((GROUP, side, side), lambda g: (jnp.minimum(g, steps - 1), 0, 0))
    pixels = count * side * side
    weights = pl.pallas_call(
        weight_body,
        grid=(steps + 1,),
        in_specs=[smem, smem, tiles],
        out_specs=pl.BlockSpec((parts, GROUP, height, side), lambda g: (0, g, 0, 0)),
        out_shape=jax.ShapeDtypeStruct((parts, slots, height, side), jnp.bfloat16),
        scratch_shapes=[pltpu.VMEM((GROUP, 2, 2 * side, side // 2), jnp.float32)],
        cost_estimate=pl.CostEstimate(flops=20 * pixels, bytes_accessed=4 * pixels, transcendentals=0),
        name="weights",
    )(tile_patch.T, tile_offset.T, tile_var)
    tile_image, weights = lax.optimization_barrier((tile_image, weights))
    values = pl.pallas_call(
        value_body,
        grid=(steps + 1,),
        in_specs=[smem] * 6 + [pl.BlockSpec((side, 3 * side), lambda g: (0, 0)), tiles, tiles],
        out_specs=[pl.BlockSpec((GROUP, 32, side), lambda g: (g, 0, 0))] * 8,
        out_shape=[jax.ShapeDtypeStruct((slots, 32, side), jnp.bfloat16)] * 8,
        scratch_shapes=[
            pltpu.VMEM((GROUP, 3, side, side), jnp.float32),
            pltpu.VMEM((GROUP, 2, 2 * side, side // 2), jnp.float32),
        ],
        cost_estimate=pl.CostEstimate(flops=12 * pixels * side, bytes_accessed=6 * pixels, transcendentals=0),
        compiler_params=pltpu.CompilerParams(vmem_limit_bytes=60 << 20),
        name="values",
    )(me, tile_patch.T, tile_offset.T, tile_visit, visit_scale, psf_coef.T, table, tile_image, tile_var)

    def share(m, rows):
        turn, other = m & 3, m >> 2
        pairs = [
            (e * parts + d, ((e + turn) % epochs) * parts + (d ^ other)) for e in range(epochs) for d in range(parts)
        ]
        return lax.ppermute(rows, ("epoch", "patch"), pairs)

    got = [values[0]] + [share(m, values[m]) if m != 4 else None for m in range(1, 8)]
    got_weights = lax.all_to_all(weights, "patch", split_axis=0, concat_axis=0, tiled=True)
    got_weights, got[1], got[2] = lax.optimization_barrier((got_weights, got[1], got[2]))
    weight_sums = pl.pallas_call(
        weight_sum_body,
        in_specs=[smem, smem, smem, vmem],
        out_specs=vmem,
        out_shape=jax.ShapeDtypeStruct((4, parts, height, side), jnp.bfloat16),
        cost_estimate=pl.CostEstimate(flops=10 * pixels, bytes_accessed=3 * pixels, transcendentals=0),
        compiler_params=pltpu.CompilerParams(vmem_limit_bytes=60 << 20),
        name="weight_sums",
    )(*by_patch(got_weights[:, count, :3, :count], slots, parts), me, got_weights.reshape(parts * slots, height, side))

    core_share, weight_sums = lax.optimization_barrier((values[4], weight_sums))
    got[4] = share(4, core_share)
    known = jnp.stack([g[count, :3, :count] for g in got])
    hbm = pl.BlockSpec(memory_space=pl.ANY)
    sums = pl.pallas_call(
        value_sum_body,
        in_specs=[smem, smem, smem, vmem] + [hbm] * 8,
        out_specs=vmem,
        out_shape=jax.ShapeDtypeStruct((4, parts, 32 + height, side), jnp.bfloat16),
        scratch_shapes=[pltpu.VMEM((8 * slots, 32, side), jnp.bfloat16), pltpu.SemaphoreType.DMA((8,))],
        cost_estimate=pl.CostEstimate(flops=10 * pixels, bytes_accessed=4 * pixels, transcendentals=0),
        compiler_params=pltpu.CompilerParams(vmem_limit_bytes=56 << 20),
        name="value_sums",
    )(*by_patch(known, slots, parts), me, weight_sums, *got)

    sums = sums.reshape(epochs * parts, 32 + height, side)
    got = lax.all_to_all(sums, ("epoch", "patch"), split_axis=0, concat_axis=0, tiled=True)
    quarter = jax.ShapeDtypeStruct((1, 4 * parts, 2 * side), jnp.float32)
    return pl.pallas_call(
        final_body,
        in_specs=[vmem],
        out_specs=(vmem, vmem),
        out_shape=(quarter, quarter),
        compiler_params=pltpu.CompilerParams(vmem_limit_bytes=32 << 20),
        name="final",
    )(got.reshape(epochs, parts, 32 + height, side))


def solution(mesh):
    placed = (
        P(("epoch", "patch"), None, None),
        P(("epoch", "patch"), None, None),
        P(("epoch", "patch"), None),
        P(("epoch", "patch"), None),
        P(("epoch", "patch"), None),
        P(("epoch", "patch")),
        P(),
    )
    return jax.shard_map(
        shards,
        mesh=mesh,
        in_specs=placed,
        out_specs=(P("patch", "epoch", None), P("patch", "epoch", None)),
        check_vma=False,
    )
```

```python
import functools

import jax
import jax.numpy as jnp
import numpy as np
from jax import lax
from jax.experimental import pallas as pl
from jax.experimental.pallas import tpu as pltpu
from jax.sharding import PartitionSpec as P

SIGMAS = (1.0, 2.0, 3.5)
REACH = 7
GROUP = 4
WEIGHT_GROUP = 8
FIRST = 12


def blur_kernels(side):
    place = np.arange(side)
    distance = (place[:, None] - place[None, :]).astype(np.float32)
    taps = np.arange(-REACH, REACH + 1).astype(np.float32)
    tables = []
    for sigma in SIGMAS:
        scale = np.float32(2.0 * sigma * sigma)
        profile = np.where(np.abs(distance) <= REACH, np.exp(-distance * distance / scale), np.float32(0.0))
        tables.append(profile / np.sum(np.exp(-taps * taps / scale), dtype=np.float32))
    return np.concatenate(tables, axis=1).astype(jnp.bfloat16)


def keep_turned(value, off_c, wide_ref, first_row):
    rows, side = value.shape
    turned = pltpu.roll(value, off_c & (side - 1), 1)
    for h in range(2):
        lanes = turned[:, h * (side // 2) : (h + 1) * (side // 2)]
        wide_ref[h, first_row : first_row + rows] = lanes
        wide_ref[h, first_row + side : first_row + side + rows] = lanes


def table_of_tiles(patch_ref, off_ref, shape):
    lane = lax.broadcasted_iota(jnp.int32, shape, 1)
    row = lax.broadcasted_iota(jnp.int32, shape, 0)
    known = jnp.zeros(shape, jnp.int32)
    for t in range(patch_ref.shape[1]):
        mine = jnp.where(row == 0, patch_ref[0, t], jnp.where(row == 1, off_ref[0, t], off_ref[1, t]))
        known = jnp.where((lane == t) & (row < 3), mine, known)
    return known.astype(jnp.float32).astype(jnp.bfloat16)


def weight_body(patch_ref, off_ref, var_ref, out_ref, wide_ref):
    parts, group, height, side = out_ref.shape
    step = pl.program_id(0)
    half, swap = side // 2, height // 2
    chunk = 32

    @pl.when(step < pl.num_programs(0) - 1)
    def _():
        first = lax.broadcasted_iota(jnp.int32, (height, half), 0) < swap
        for t in range(group):
            tile = step * group + t
            off_r, off_c = off_ref[0, tile], off_ref[1, tile]
            for c in range(side // chunk):
                weight = 1.0 / var_ref[t, c * chunk : (c + 1) * chunk].astype(jnp.float32)
                keep_turned(weight, off_c, wide_ref.at[t], c * chunk)
            for part in range(parts):
                begins = [(4 * part - off_r) & (side - 1), (half + 4 * part - swap - off_r) & (side - 1)]
                for h in range(2):
                    rows = [wide_ref[t, h, pl.ds(begin, height)] for begin in begins]
                    out_ref[part, t, :, h * half : (h + 1) * half] = jnp.where(first, *rows).astype(jnp.bfloat16)

    @pl.when(step == pl.num_programs(0) - 1)
    def _():
        known = table_of_tiles(patch_ref, off_ref, (height, side))
        for part in range(parts):
            out_ref[part, 0] = known


def value_body(begin, tables, me_ref, patch_ref, off_ref, visit_ref, scale_ref, coef_ref, kernel_ref, image_ref, var_ref, *refs):
    outs, (blur_ref, wide_ref) = refs[:8], refs[8:]
    group, height, side = outs[0].shape
    step = pl.program_id(0)
    half, band = side // 2, height // 2
    chunk = 32

    @pl.when(step < pl.num_programs(0) - tables)
    def _():
        lane = lax.broadcasted_iota(jnp.int32, (chunk, half), 1)
        row = lax.broadcasted_iota(jnp.int32, (chunk, half), 0)
        xs = [(2.0 * (lane + h * half).astype(jnp.float32) + 1.0) / side - 1.0 for h in range(2)]
        for t in range(group):
            tile = begin + step * group + t
            off_r, off_c = off_ref[0, tile], off_ref[1, tile]
            gain = scale_ref[visit_ref[tile]]
            k = [[coef_ref[6 * b + j, tile] for j in range(6)] for b in range(3)]
            square = [[k[b][5] * x for x in xs] for b in range(3)]
            row_pass = jnp.dot(image_ref[t], kernel_ref[...], preferred_element_type=jnp.float32).astype(jnp.bfloat16)
            for b in range(3):
                cols = slice(b * side, (b + 1) * side)
                blur_ref[t, b] = jnp.dot(kernel_ref[:, cols], row_pass[:, cols], preferred_element_type=jnp.float32)
            for c in range(side // chunk):
                rows = slice(c * chunk, (c + 1) * chunk)
                y = (2.0 * (row + c * chunk).astype(jnp.float32) + 1.0) / side - 1.0
                level = [k[b][0] + y * (k[b][1] + k[b][3] * y) for b in range(3)]
                slope = [k[b][2] + k[b][4] * y for b in range(3)]
                both = []
                for h in range(2):
                    cols = slice(h * half, (h + 1) * half)
                    matched = None
                    for b in range(3):
                        spatial = level[b] + xs[h] * (slope[b] + square[b][h])
                        term = spatial * blur_ref[t, b, rows, cols]
                        matched = term if matched is None else matched + term
                    both.append(gain * (1.0 / var_ref[t, rows, cols].astype(jnp.float32)) * matched)
                keep_turned(jnp.concatenate(both, axis=1), off_c, wide_ref.at[t], c * chunk)
            for m in range(8):
                member = (((me_ref[0] + (m & 3)) & 3) << 1) + (me_ref[1] ^ (m >> 2))
                for part in range(2):
                    top = (part * half + (member << 4) - off_r) & (side - 1)
                    for h in range(2):
                        rows = wide_ref[t, h, pl.ds(top, band)]
                        outs[m][t, part * band : (part + 1) * band, h * half : (h + 1) * half] = rows.astype(jnp.bfloat16)

    if tables:

        @pl.when(step == pl.num_programs(0) - 1)
        def _():
            known = table_of_tiles(patch_ref, off_ref, (height, side))
            for m in range(8):
                outs[m][0] = known


def clear_sums(sums_ref):
    zero = jnp.zeros(sums_ref.shape[1:], jnp.float32)

    def clear(p, unused):
        sums_ref[p] = zero
        return unused

    lax.fori_loop(0, sums_ref.shape[0], clear, 0)


def weight_sum_body(known_ref, me_ref, got_ref, out_ref, data_ref, sems, *sums_refs):
    sources, slots, height, side = got_ref.shape
    tiles, patches = slots - 1, out_ref.shape[1]
    bunch = sources // sems.shape[0]
    copies = [
        pltpu.make_async_copy(got_ref.at[pl.ds(n * bunch, bunch)], data_ref.at[pl.ds(n * bunch, bunch)], sems.at[n])
        for n in range(sems.shape[0])
    ]
    for copy in copies:
        copy.start()
    s = lax.broadcasted_iota(jnp.int32, (height, side), 0)
    row = (s >> 2) * (side // 2) + 4 * me_ref[2] + (s & 3)
    lane = lax.broadcasted_iota(jnp.int32, (height, side), 1)
    swap = height // 2
    first = s < swap
    for sums_ref in sums_refs:
        clear_sums(sums_ref)

    def add_source(source, unused):
        for t in range(tiles):
            p, off_r, off_c = known_ref[source, 0, t], known_ref[source, 1, t], known_ref[source, 2, t]
            sums_ref = sums_refs[t % len(sums_refs)]
            value = data_ref[source, t].astype(jnp.float32)
            left = jnp.where(lane >= off_c, value, 0.0)
            right = value - left
            upper = row >= off_r
            upper_left, upper_right = jnp.where(upper, left, 0.0), jnp.where(upper, right, 0.0)
            sums_ref[p, 0] += upper_left
            sums_ref[p, 1] += upper_right
            sums_ref[p, 2] += left - upper_left
            sums_ref[p, 3] += right - upper_right
        return unused

    for n, copy in enumerate(copies):
        copy.wait()
        lax.fori_loop(n * bunch, (n + 1) * bunch, add_source, 0)

    def one_patch(p, unused):
        for half in range(2):
            left, right = (sum(sums_ref[p, 2 * half + h] for sums_ref in sums_refs) for h in range(2))
            out_ref[2 * half, p] = jnp.where(first, left, pltpu.roll(right, swap, 0)).astype(jnp.bfloat16)
            out_ref[2 * half + 1, p] = jnp.where(first, pltpu.roll(left, swap, 0), right).astype(jnp.bfloat16)
        return unused

    lax.fori_loop(0, patches, one_patch, 0)


def add_values(known_ref, me_ref, begin, tiles, copies, data_ref, sums_ref):
    _, _, height, side = data_ref.shape
    band = height // 2
    s = lax.broadcasted_iota(jnp.int32, (band, side), 0) + (((me_ref[0] << 1) + me_ref[1]) << 4)
    lane = lax.broadcasted_iota(jnp.int32, (band, side), 1)

    for m, copy in enumerate(copies):
        copy.wait()

        def some_tiles(step, unused):
            for u in range(4):
                t = 4 * step + u
                p, off_r, off_c = (known_ref[m, n, begin + t] for n in range(3))
                for part in range(2):
                    value = data_ref[m, t, part * band : (part + 1) * band].astype(jnp.float32)
                    left = jnp.where(lane >= off_c, value, 0.0)
                    right = value - left
                    upper = s >= off_r - part * (side // 2)
                    upper_left, upper_right = jnp.where(upper, left, 0.0), jnp.where(upper, right, 0.0)
                    sums_ref[p, part, 0] += upper_left
                    sums_ref[p, part, 1] += upper_right
                    sums_ref[p, 2 + part, 0] += left - upper_left
                    sums_ref[p, 2 + part, 1] += right - upper_right
            return unused

        lax.fori_loop(0, tiles // 4, some_tiles, 0)


def first_values_body(known_ref, me_ref, *refs):
    got, out_ref, (data_ref, sems) = refs[:8], refs[8], refs[9:]
    tiles = got[0].shape[0] - 1
    copies = [pltpu.make_async_copy(got[m].at[pl.ds(0, tiles)], data_ref.at[m], sems.at[m]) for m in range(8)]
    for copy in copies:
        copy.start()
    clear_sums(out_ref)
    add_values(known_ref, me_ref, 0, tiles, copies, data_ref, out_ref)


def last_values_body(known_ref, me_ref, weight_ref, before_ref, *refs):
    got, out_ref, (data_ref, first_ref, sums_ref, sems, first_sem) = refs[:8], refs[8], refs[9:]
    tiles = got[0].shape[0]
    band = sums_ref.shape[3]
    copies = [pltpu.make_async_copy(got[m], data_ref.at[m], sems.at[m]) for m in range(8)]
    for copy in copies:
        copy.start()
    earlier = pltpu.make_async_copy(before_ref, first_ref, first_sem)
    earlier.start()
    clear_sums(sums_ref)
    add_values(known_ref, me_ref, known_ref.shape[2] - tiles, tiles, copies, data_ref, sums_ref)
    earlier.wait()

    def one_patch(p, unused):
        for quarter in range(4):
            for h in range(2):
                both = sums_ref[p, quarter, h] + first_ref[p, quarter, h]
                out_ref[quarter, p, h * band : (h + 1) * band] = both.astype(jnp.bfloat16)
            out_ref[quarter, p, 2 * band :] = weight_ref[quarter, p]
        return unused

    lax.fori_loop(0, out_ref.shape[1], one_patch, 0)


def final_body(got_ref, value_ref, weight_ref):
    epochs, parts, height, side = got_ref.shape
    band = 16
    for z in range(epochs):
        for core in range(2):
            rows = slice((2 * z + core) * band, (2 * z + core + 1) * band)
            for h in range(2):
                total = jnp.zeros((band, side), jnp.float32)
                for chip in range(parts // 2):
                    total += got_ref[z, 2 * chip + core, h * band : (h + 1) * band].astype(jnp.float32)
                value_ref[0, rows, h * side : (h + 1) * side] = total
    swap = 4
    first = lax.broadcasted_iota(jnp.int32, (8, side), 0) < swap
    for pair in range(parts // 2):
        both = []
        for part in (2 * pair, 2 * pair + 1):
            total = got_ref[0, part, 2 * band :].astype(jnp.float32)
            for e in range(1, epochs):
                total += got_ref[e, part, 2 * band :].astype(jnp.float32)
            both.append(total)
        rows = slice(pair * 8, (pair + 1) * 8)
        weight_ref[0, rows, :side] = jnp.where(first, both[0], pltpu.roll(both[1], swap, 0))
        weight_ref[0, rows, side:] = jnp.where(first, pltpu.roll(both[0], swap, 0), both[1])


def shards(tile_image, tile_var, psf_coef, tile_patch, tile_offset, tile_visit, visit_scale):
    count, side = tile_image.shape[:2]
    parts = lax.axis_size("patch")
    epochs = lax.axis_size("epoch")
    height = side // parts
    slots = count + 1
    z, j = lax.axis_index("epoch"), lax.axis_index("patch")
    me = jnp.stack([z, j & 1, j]).astype(jnp.int32)
    table = jnp.asarray(blur_kernels(side))

    smem = pl.BlockSpec(memory_space=pltpu.SMEM)
    vmem = pl.BlockSpec(memory_space=pltpu.VMEM)
    steps = count // WEIGHT_GROUP
    tiles = pl.BlockSpec((WEIGHT_GROUP, side, side), lambda g: (jnp.minimum(g, steps - 1), 0, 0))
    pixels = count * side * side
    weights = pl.pallas_call(
        weight_body,
        grid=(steps + 1,),
        in_specs=[smem, smem, tiles],
        out_specs=pl.BlockSpec((parts, WEIGHT_GROUP, height, side), lambda g: (0, g, 0, 0)),
        out_shape=jax.ShapeDtypeStruct((parts, slots, height, side), jnp.bfloat16),
        scratch_shapes=[pltpu.VMEM((WEIGHT_GROUP, 2, 2 * side, side // 2), jnp.float32)],
        cost_estimate=pl.CostEstimate(flops=20 * pixels, bytes_accessed=4 * pixels, transcendentals=0),
        compiler_params=pltpu.CompilerParams(vmem_limit_bytes=60 << 20),
        name="weights",
    )(tile_patch.T, tile_offset.T, tile_var)
    def some_values(begin, end, tables, image):
        steps, group = (end - begin) // GROUP, begin // GROUP
        taken = pl.BlockSpec((GROUP, side, side), lambda g: (group + jnp.minimum(g, steps - 1), 0, 0))
        return pl.pallas_call(
            functools.partial(value_body, begin, tables),
            grid=(steps + tables,),
            in_specs=[smem] * 6 + [pl.BlockSpec((side, 3 * side), lambda g: (0, 0)), taken, taken],
            out_specs=[pl.BlockSpec((GROUP, 32, side), lambda g: (g, 0, 0))] * 8,
            out_shape=[jax.ShapeDtypeStruct((end - begin + tables, 32, side), jnp.bfloat16)] * 8,
            scratch_shapes=[
                pltpu.VMEM((GROUP, 3, side, side), jnp.float32),
                pltpu.VMEM((GROUP, 2, 2 * side, side // 2), jnp.float32),
            ],
            cost_estimate=pl.CostEstimate(flops=6 * pixels * side, bytes_accessed=3 * pixels, transcendentals=0),
            compiler_params=pltpu.CompilerParams(vmem_limit_bytes=60 << 20),
            name="values",
        )(me, tile_patch.T, tile_offset.T, tile_visit, visit_scale, psf_coef.T, table, image, tile_var)

    def share(m, rows):
        turn, other = m & 3, m >> 2
        pairs = [
            (e * parts + d, ((e + turn) % epochs) * parts + (d ^ other)) for e in range(epochs) for d in range(parts)
        ]
        return lax.ppermute(rows, ("epoch", "patch"), pairs)

    ints = lambda rows: rows.astype(jnp.float32).astype(jnp.int32)
    hbm = pl.BlockSpec(memory_space=pl.ANY)
    mine = jax.ShapeDtypeStruct((parts, 4, 2, 16, side), jnp.float32)
    tile_image, weights = lax.optimization_barrier((tile_image, weights))
    got_weights = lax.all_to_all(weights, "patch", split_axis=0, concat_axis=0, tiled=True)

    early = some_values(0, FIRST, 1, tile_image)
    got = {0: early[0]}
    for m in (1, 3, 2, 7, 5, 6, 4):
        got[m] = share(m, early[m])
    got = [got[m] for m in range(8)]
    tile_image, early_0 = lax.optimization_barrier((tile_image, early[0]))
    late = some_values(FIRST, count, 0, tile_image)
    more = {0: late[0]}
    for m in (1, 3, 2, 7, 5):
        more[m] = share(m, late[m])
    known = ints(jnp.stack([g[FIRST, :3, :count] for g in got]))
    value_sums = pl.pallas_call(
        first_values_body,
        in_specs=[smem, smem] + [hbm] * 8,
        out_specs=vmem,
        out_shape=mine,
        scratch_shapes=[pltpu.VMEM((8, FIRST, 32, side), jnp.bfloat16), pltpu.SemaphoreType.DMA((8,))],
        cost_estimate=pl.CostEstimate(flops=5 * pixels, bytes_accessed=3 * pixels, transcendentals=0),
        compiler_params=pltpu.CompilerParams(vmem_limit_bytes=56 << 20),
        name="first_value_sums",
    )(known, me, *got)

    late_6, late_4, value_sums = lax.optimization_barrier((late[6], late[4], value_sums))
    more[6], more[4] = share(6, late_6), share(4, late_4)
    got_weights, more[1], more[3], value_sums = lax.optimization_barrier((got_weights, more[1], more[3], value_sums))
    weight_sums = pl.pallas_call(
        weight_sum_body,
        in_specs=[smem, smem, hbm],
        out_specs=vmem,
        out_shape=jax.ShapeDtypeStruct((4, parts, height, side), jnp.bfloat16),
        scratch_shapes=[
            pltpu.VMEM((parts, slots, height, side), jnp.bfloat16),
            pltpu.SemaphoreType.DMA((4,)),
            *[pltpu.VMEM((parts, 4, height, side), jnp.float32)] * 4,
        ],
        cost_estimate=pl.CostEstimate(flops=10 * pixels, bytes_accessed=3 * pixels, transcendentals=0),
        compiler_params=pltpu.CompilerParams(vmem_limit_bytes=60 << 20),
        name="weight_sums",
    )(ints(got_weights[:, count, :3, :count]), me, got_weights)
    sums = pl.pallas_call(
        last_values_body,
        in_specs=[smem, smem, vmem, hbm] + [hbm] * 8,
        out_specs=vmem,
        out_shape=jax.ShapeDtypeStruct((4, parts, 32 + height, side), jnp.bfloat16),
        scratch_shapes=[
            pltpu.VMEM((8, count - FIRST, 32, side), jnp.bfloat16),
            pltpu.VMEM(mine.shape, jnp.float32),
            pltpu.VMEM(mine.shape, jnp.float32),
            pltpu.SemaphoreType.DMA((8,)),
            pltpu.SemaphoreType.DMA,
        ],
        cost_estimate=pl.CostEstimate(flops=5 * pixels, bytes_accessed=3 * pixels, transcendentals=0),
        compiler_params=pltpu.CompilerParams(vmem_limit_bytes=56 << 20),
        name="last_value_sums",
    )(known, me, weight_sums, value_sums, *[more[m] for m in range(8)])

    sums = sums.reshape(epochs * parts, 32 + height, side)
    got = lax.all_to_all(sums, ("epoch", "patch"), split_axis=0, concat_axis=0, tiled=True)
    quarter = jax.ShapeDtypeStruct((1, 4 * parts, 2 * side), jnp.float32)
    return pl.pallas_call(
        final_body,
        in_specs=[vmem],
        out_specs=(vmem, vmem),
        out_shape=(quarter, quarter),
        compiler_params=pltpu.CompilerParams(vmem_limit_bytes=32 << 20),
        name="final",
    )(got.reshape(epochs, parts, 32 + height, side))


def solution(mesh):
    placed = (
        P(("epoch", "patch"), None, None),
        P(("epoch", "patch"), None, None),
        P(("epoch", "patch"), None),
        P(("epoch", "patch"), None),
        P(("epoch", "patch"), None),
        P(("epoch", "patch")),
        P(),
    )
    return jax.shard_map(
        shards,
        mesh=mesh,
        in_specs=placed,
        out_specs=(P("patch", "epoch", None), P("patch", "epoch", None)),
        check_vma=False,
    )
```

```python
import functools

import jax
import jax.numpy as jnp
import numpy as np
from jax import lax
from jax.experimental import pallas as pl
from jax.experimental.pallas import tpu as pltpu
from jax.sharding import PartitionSpec as P

SIGMAS = (1.0, 2.0, 3.5)
REACH = 7
GROUP = 4
WEIGHT_GROUP = 8
FIRST = 12
EARLY = (0,)


def blur_kernels(side):
    place = np.arange(side)
    distance = (place[:, None] - place[None, :]).astype(np.float32)
    taps = np.arange(-REACH, REACH + 1).astype(np.float32)
    tables = []
    for sigma in SIGMAS:
        scale = np.float32(2.0 * sigma * sigma)
        profile = np.where(np.abs(distance) <= REACH, np.exp(-distance * distance / scale), np.float32(0.0))
        tables.append(profile / np.sum(np.exp(-taps * taps / scale), dtype=np.float32))
    return np.concatenate(tables, axis=1).astype(jnp.bfloat16)


def keep_turned(value, off_c, wide_ref, first_row):
    rows, side = value.shape
    turned = pltpu.roll(value, off_c & (side - 1), 1)
    for h in range(2):
        lanes = turned[:, h * (side // 2) : (h + 1) * (side // 2)]
        wide_ref[h, first_row : first_row + rows] = lanes
        wide_ref[h, first_row + side : first_row + side + rows] = lanes


def table_of_tiles(patch_ref, off_ref, shape):
    lane = lax.broadcasted_iota(jnp.int32, shape, 1)
    row = lax.broadcasted_iota(jnp.int32, shape, 0)
    known = jnp.zeros(shape, jnp.int32)
    for t in range(patch_ref.shape[1]):
        mine = jnp.where(row == 0, patch_ref[0, t], jnp.where(row == 1, off_ref[0, t], off_ref[1, t]))
        known = jnp.where((lane == t) & (row < 3), mine, known)
    return known.astype(jnp.float32).astype(jnp.bfloat16)


def weight_body(patch_ref, off_ref, var_ref, out_ref, wide_ref):
    parts, group, height, side = out_ref.shape
    step = pl.program_id(0)
    half, swap = side // 2, height // 2
    chunk = 32

    @pl.when(step < pl.num_programs(0) - 1)
    def _():
        first = lax.broadcasted_iota(jnp.int32, (height, half), 0) < swap
        for t in range(group):
            tile = step * group + t
            off_r, off_c = off_ref[0, tile], off_ref[1, tile]
            for c in range(side // chunk):
                weight = 1.0 / var_ref[t, c * chunk : (c + 1) * chunk].astype(jnp.float32)
                keep_turned(weight, off_c, wide_ref.at[t], c * chunk)
            for part in range(parts):
                begins = [(4 * part - off_r) & (side - 1), (half + 4 * part - swap - off_r) & (side - 1)]
                for h in range(2):
                    rows = [wide_ref[t, h, pl.ds(begin, height)] for begin in begins]
                    out_ref[part, t, :, h * half : (h + 1) * half] = jnp.where(first, *rows).astype(jnp.bfloat16)

    @pl.when(step == pl.num_programs(0) - 1)
    def _():
        known = table_of_tiles(patch_ref, off_ref, (height, side))
        for part in range(parts):
            out_ref[part, 0] = known


def value_body(begin, tables, z_ref, core_ref, patch_ref, off_ref, visit_ref, scale_ref, coef_ref, kernel_ref, image_ref, var_ref, *refs):
    outs, (blur_ref, wide_ref) = refs[:8], refs[8:]
    group, height, side = outs[0].shape
    step = pl.program_id(0)
    half, band = side // 2, height // 2
    chunk = 32

    @pl.when(step < pl.num_programs(0) - tables)
    def _():
        lane = lax.broadcasted_iota(jnp.int32, (chunk, half), 1)
        row = lax.broadcasted_iota(jnp.int32, (chunk, half), 0)
        xs = [(2.0 * (lane + h * half).astype(jnp.float32) + 1.0) / side - 1.0 for h in range(2)]
        for t in range(group):
            tile = begin + step * group + t
            off_r, off_c = off_ref[0, tile], off_ref[1, tile]
            gain = scale_ref[visit_ref[tile]]
            k = [[coef_ref[6 * b + j, tile] for j in range(6)] for b in range(3)]
            square = [[k[b][5] * x for x in xs] for b in range(3)]
            row_pass = jnp.dot(image_ref[t], kernel_ref[...], preferred_element_type=jnp.float32).astype(jnp.bfloat16)
            for b in range(3):
                cols = slice(b * side, (b + 1) * side)
                blur_ref[t, b] = jnp.dot(kernel_ref[:, cols], row_pass[:, cols], preferred_element_type=jnp.float32)
            for c in range(side // chunk):
                rows = slice(c * chunk, (c + 1) * chunk)
                y = (2.0 * (row + c * chunk).astype(jnp.float32) + 1.0) / side - 1.0
                level = [k[b][0] + y * (k[b][1] + k[b][3] * y) for b in range(3)]
                slope = [k[b][2] + k[b][4] * y for b in range(3)]
                both = []
                for h in range(2):
                    cols = slice(h * half, (h + 1) * half)
                    matched = None
                    for b in range(3):
                        spatial = level[b] + xs[h] * (slope[b] + square[b][h])
                        term = spatial * blur_ref[t, b, rows, cols]
                        matched = term if matched is None else matched + term
                    both.append(gain * (1.0 / var_ref[t, rows, cols].astype(jnp.float32)) * matched)
                keep_turned(jnp.concatenate(both, axis=1), off_c, wide_ref.at[t], c * chunk)
            for m in range(8):
                member = (((z_ref[0] + (m & 3)) & 3) << 1) + (core_ref[0] ^ (m >> 2))
                for part in range(2):
                    top = (part * half + (member << 4) - off_r) & (side - 1)
                    for h in range(2):
                        rows = wide_ref[t, h, pl.ds(top, band)]
                        outs[m][t, part * band : (part + 1) * band, h * half : (h + 1) * half] = rows.astype(jnp.bfloat16)

    if tables:

        @pl.when(step == pl.num_programs(0) - 1)
        def _():
            known = table_of_tiles(patch_ref, off_ref, (height, side))
            for m in range(8):
                outs[m][0] = known


def clear_sums(sums_ref):
    zero = jnp.zeros(sums_ref.shape[1:], jnp.float32)

    def clear(p, unused):
        sums_ref[p] = zero
        return unused

    lax.fori_loop(0, sums_ref.shape[0], clear, 0)


def weight_sum_body(known_ref, part_ref, got_ref, out_ref, data_ref, sems, *sums_refs):
    sources, slots, height, side = got_ref.shape
    tiles, patches = slots - 1, out_ref.shape[1]
    bunch = sources // sems.shape[0]
    copies = [
        pltpu.make_async_copy(got_ref.at[pl.ds(n * bunch, bunch)], data_ref.at[pl.ds(n * bunch, bunch)], sems.at[n])
        for n in range(sems.shape[0])
    ]
    for copy in copies:
        copy.start()
    s = lax.broadcasted_iota(jnp.int32, (height, side), 0)
    row = (s >> 2) * (side // 2) + 4 * part_ref[0] + (s & 3)
    lane = lax.broadcasted_iota(jnp.int32, (height, side), 1)
    swap = height // 2
    first = s < swap
    for sums_ref in sums_refs:
        clear_sums(sums_ref)

    def add_source(source, unused):
        for t in range(tiles):
            p, off_r, off_c = known_ref[source, 0, t], known_ref[source, 1, t], known_ref[source, 2, t]
            sums_ref = sums_refs[t % len(sums_refs)]
            value = data_ref[source, t].astype(jnp.float32)
            left = jnp.where(lane >= off_c, value, 0.0)
            right = value - left
            upper = row >= off_r
            upper_left, upper_right = jnp.where(upper, left, 0.0), jnp.where(upper, right, 0.0)
            sums_ref[p, 0] += upper_left
            sums_ref[p, 1] += upper_right
            sums_ref[p, 2] += left - upper_left
            sums_ref[p, 3] += right - upper_right
        return unused

    for n, copy in enumerate(copies):
        copy.wait()
        lax.fori_loop(n * bunch, (n + 1) * bunch, add_source, 0)

    def one_patch(p, unused):
        for half in range(2):
            left, right = (sum(sums_ref[p, 2 * half + h] for sums_ref in sums_refs) for h in range(2))
            out_ref[2 * half, p] = jnp.where(first, left, pltpu.roll(right, swap, 0)).astype(jnp.bfloat16)
            out_ref[2 * half + 1, p] = jnp.where(first, pltpu.roll(left, swap, 0), right).astype(jnp.bfloat16)
        return unused

    lax.fori_loop(0, patches, one_patch, 0)


def add_values(known_ref, z_ref, core_ref, shares, got, data_ref, sums_ref, sems):
    _, _, height, side = data_ref.shape
    band = height // 2
    copies = [
        pltpu.make_async_copy(rows.at[pl.ds(0, tiles)], data_ref.at[n, pl.ds(0, tiles)], sems.at[n])
        for n, (rows, (m, begin, tiles)) in enumerate(zip(got, shares))
    ]
    for copy in copies:
        copy.start()
    zero = jnp.zeros(sums_ref.shape[1:], jnp.float32)

    def clear(p, unused):
        sums_ref[p] = zero
        return unused

    lax.fori_loop(0, sums_ref.shape[0], clear, 0)
    s = lax.broadcasted_iota(jnp.int32, (band, side), 0) + (((z_ref[0] << 1) + core_ref[0]) << 4)
    lane = lax.broadcasted_iota(jnp.int32, (band, side), 1)

    for n, (m, begin, tiles) in enumerate(shares):
        copies[n].wait()

        def some_tiles(step, unused):
            for u in range(4):
                t = 4 * step + u
                p, off_r, off_c = (known_ref[m, k, begin + t] for k in range(3))
                for part in range(2):
                    value = data_ref[n, t, part * band : (part + 1) * band].astype(jnp.float32)
                    left = jnp.where(lane >= off_c, value, 0.0)
                    right = value - left
                    upper = s >= off_r - part * (side // 2)
                    upper_left, upper_right = jnp.where(upper, left, 0.0), jnp.where(upper, right, 0.0)
                    sums_ref[p, part, 0] += upper_left
                    sums_ref[p, part, 1] += upper_right
                    sums_ref[p, 2 + part, 0] += left - upper_left
                    sums_ref[p, 2 + part, 1] += right - upper_right
            return unused

        lax.fori_loop(0, tiles // 4, some_tiles, 0)


def first_values_body(shares, known_ref, z_ref, core_ref, *refs):
    got, (out_ref, data_ref, sems) = refs[: len(shares)], refs[len(shares) :]
    add_values(known_ref, z_ref, core_ref, shares, got, data_ref, out_ref, sems)


def last_values_body(shares, known_ref, z_ref, core_ref, weight_ref, before_ref, *refs):
    got, (out_ref, data_ref, first_ref, sums_ref, sems, first_sem) = refs[: len(shares)], refs[len(shares) :]
    band = sums_ref.shape[3]
    earlier = pltpu.make_async_copy(before_ref, first_ref, first_sem)
    earlier.start()
    add_values(known_ref, z_ref, core_ref, shares, got, data_ref, sums_ref, sems)
    earlier.wait()

    def one_patch(p, unused):
        for quarter in range(4):
            for h in range(2):
                both = sums_ref[p, quarter, h] + first_ref[p, quarter, h]
                out_ref[quarter, p, h * band : (h + 1) * band] = both.astype(jnp.bfloat16)
            out_ref[quarter, p, 2 * band :] = weight_ref[quarter, p]
        return unused

    lax.fori_loop(0, out_ref.shape[1], one_patch, 0)


def final_body(got_ref, value_ref, weight_ref):
    epochs, parts, height, side = got_ref.shape
    band = 16
    for z in range(epochs):
        for core in range(2):
            rows = slice((2 * z + core) * band, (2 * z + core + 1) * band)
            for h in range(2):
                total = jnp.zeros((band, side), jnp.float32)
                for chip in range(parts // 2):
                    total += got_ref[z, 2 * chip + core, h * band : (h + 1) * band].astype(jnp.float32)
                value_ref[0, rows, h * side : (h + 1) * side] = total
    swap = 4
    first = lax.broadcasted_iota(jnp.int32, (8, side), 0) < swap
    for pair in range(parts // 2):
        both = []
        for part in (2 * pair, 2 * pair + 1):
            total = got_ref[0, part, 2 * band :].astype(jnp.float32)
            for e in range(1, epochs):
                total += got_ref[e, part, 2 * band :].astype(jnp.float32)
            both.append(total)
        rows = slice(pair * 8, (pair + 1) * 8)
        weight_ref[0, rows, :side] = jnp.where(first, both[0], pltpu.roll(both[1], swap, 0))
        weight_ref[0, rows, side:] = jnp.where(first, pltpu.roll(both[0], swap, 0), both[1])


def shards(tile_image, tile_var, psf_coef, tile_patch, tile_offset, tile_visit, visit_scale):
    count, side = tile_image.shape[:2]
    parts = lax.axis_size("patch")
    epochs = lax.axis_size("epoch")
    height = side // parts
    slots = count + 1
    z, j = lax.axis_index("epoch"), lax.axis_index("patch")
    place = [jnp.reshape(n, (1,)).astype(jnp.int32) for n in (z, j & 1, j)]
    table = jnp.asarray(blur_kernels(side))

    smem = pl.BlockSpec(memory_space=pltpu.SMEM)
    vmem = pl.BlockSpec(memory_space=pltpu.VMEM)
    steps = count // WEIGHT_GROUP
    tiles = pl.BlockSpec((WEIGHT_GROUP, side, side), lambda g: (jnp.minimum(g, steps - 1), 0, 0))
    pixels = count * side * side
    weights = pl.pallas_call(
        weight_body,
        grid=(steps + 1,),
        in_specs=[smem, smem, tiles],
        out_specs=pl.BlockSpec((parts, WEIGHT_GROUP, height, side), lambda g: (0, g, 0, 0)),
        out_shape=jax.ShapeDtypeStruct((parts, slots, height, side), jnp.bfloat16),
        scratch_shapes=[pltpu.VMEM((WEIGHT_GROUP, 2, 2 * side, side // 2), jnp.float32)],
        cost_estimate=pl.CostEstimate(flops=20 * pixels, bytes_accessed=4 * pixels, transcendentals=0),
        compiler_params=pltpu.CompilerParams(vmem_limit_bytes=60 << 20),
        name="weights",
    )(tile_patch.T, tile_offset.T, tile_var)
    def some_values(begin, end, tables, image):
        steps, group = (end - begin) // GROUP, begin // GROUP
        taken = pl.BlockSpec((GROUP, side, side), lambda g: (group + jnp.minimum(g, steps - 1), 0, 0))
        return pl.pallas_call(
            functools.partial(value_body, begin, tables),
            grid=(steps + tables,),
            in_specs=[smem] * 7 + [pl.BlockSpec((side, 3 * side), lambda g: (0, 0)), taken, taken],
            out_specs=[pl.BlockSpec((GROUP, 32, side), lambda g: (g, 0, 0))] * 8,
            out_shape=[jax.ShapeDtypeStruct((end - begin + tables, 32, side), jnp.bfloat16)] * 8,
            scratch_shapes=[
                pltpu.VMEM((GROUP, 3, side, side), jnp.float32),
                pltpu.VMEM((GROUP, 2, 2 * side, side // 2), jnp.float32),
            ],
            cost_estimate=pl.CostEstimate(flops=6 * pixels * side, bytes_accessed=3 * pixels, transcendentals=0),
            compiler_params=pltpu.CompilerParams(vmem_limit_bytes=60 << 20),
            name="values",
        )(*place[:2], tile_patch.T, tile_offset.T, tile_visit, visit_scale, psf_coef.T, table, image, tile_var)

    def share(m, rows):
        turn, other = m & 3, m >> 2
        pairs = [
            (e * parts + d, ((e + turn) % epochs) * parts + (d ^ other)) for e in range(epochs) for d in range(parts)
        ]
        return lax.ppermute(rows, ("epoch", "patch"), pairs)

    ints = lambda rows: rows.astype(jnp.float32).astype(jnp.int32)
    hbm = pl.BlockSpec(memory_space=pl.ANY)
    mine = jax.ShapeDtypeStruct((parts, 4, 2, 16, side), jnp.float32)
    tile_image, weights = lax.optimization_barrier((tile_image, weights))
    got_weights = lax.all_to_all(weights, "patch", split_axis=0, concat_axis=0, tiled=True)

    early = some_values(0, FIRST, 1, tile_image)
    got = {0: early[0]}
    for m in (1, 3, 2, 7, 5, 6, 4):
        got[m] = share(m, early[m])
    got = [got[m] for m in range(8)]
    tile_image, early_0 = lax.optimization_barrier((tile_image, early[0]))
    late = some_values(FIRST, count, 0, tile_image)
    more = {0: late[0]}
    for m in (1, 3, 2, 7, 5, 6):
        more[m] = share(m, late[m])
    known = ints(jnp.stack([g[FIRST, :3, :count] for g in got]))
    shares = [(m, 0, FIRST) for m in range(8)] + [(m, FIRST, count - FIRST) for m in EARLY]
    more[1], got[0], late_4 = lax.optimization_barrier((more[1], got[0], late[4]))
    value_sums = pl.pallas_call(
        functools.partial(first_values_body, shares),
        in_specs=[smem] * 3 + [hbm] * len(shares),
        out_specs=vmem,
        out_shape=mine,
        scratch_shapes=[
            pltpu.VMEM((len(shares), count - FIRST, 32, side), jnp.bfloat16),
            pltpu.SemaphoreType.DMA((len(shares),)),
        ],
        cost_estimate=pl.CostEstimate(flops=5 * pixels, bytes_accessed=3 * pixels, transcendentals=0),
        compiler_params=pltpu.CompilerParams(vmem_limit_bytes=56 << 20),
        name="first_value_sums",
    )(known, *place[:2], *got, *[more[m] for m in EARLY])

    late_4, value_sums = lax.optimization_barrier((late_4, value_sums))
    more[4] = share(4, late_4)
    got_weights, value_sums = lax.optimization_barrier((got_weights, value_sums))
    weight_sums = pl.pallas_call(
        weight_sum_body,
        in_specs=[smem, smem, hbm],
        out_specs=vmem,
        out_shape=jax.ShapeDtypeStruct((4, parts, height, side), jnp.bfloat16),
        scratch_shapes=[
            pltpu.VMEM((parts, slots, height, side), jnp.bfloat16),
            pltpu.SemaphoreType.DMA((8,)),
            *[pltpu.VMEM((parts, 4, height, side), jnp.float32)] * 4,
        ],
        cost_estimate=pl.CostEstimate(flops=10 * pixels, bytes_accessed=3 * pixels, transcendentals=0),
        compiler_params=pltpu.CompilerParams(vmem_limit_bytes=60 << 20),
        name="weight_sums",
    )(ints(got_weights[:, count, :3, :count]), place[2], got_weights)
    shares = [(m, FIRST, count - FIRST) for m in range(8) if m not in EARLY]
    sums = pl.pallas_call(
        functools.partial(last_values_body, shares),
        in_specs=[smem] * 3 + [vmem, hbm] + [hbm] * len(shares),
        out_specs=vmem,
        out_shape=jax.ShapeDtypeStruct((4, parts, 32 + height, side), jnp.bfloat16),
        scratch_shapes=[
            pltpu.VMEM((len(shares), count - FIRST, 32, side), jnp.bfloat16),
            pltpu.VMEM(mine.shape, jnp.float32),
            pltpu.VMEM(mine.shape, jnp.float32),
            pltpu.SemaphoreType.DMA((len(shares),)),
            pltpu.SemaphoreType.DMA,
        ],
        cost_estimate=pl.CostEstimate(flops=5 * pixels, bytes_accessed=3 * pixels, transcendentals=0),
        compiler_params=pltpu.CompilerParams(vmem_limit_bytes=56 << 20),
        name="last_value_sums",
    )(known, *place[:2], weight_sums, value_sums, *[more[m] for m, _, _ in shares])

    sums = sums.reshape(epochs * parts, 32 + height, side)
    got = lax.all_to_all(sums, ("epoch", "patch"), split_axis=0, concat_axis=0, tiled=True)
    quarter = jax.ShapeDtypeStruct((1, 4 * parts, 2 * side), jnp.float32)
    return pl.pallas_call(
        final_body,
        in_specs=[vmem],
        out_specs=(vmem, vmem),
        out_shape=(quarter, quarter),
        compiler_params=pltpu.CompilerParams(vmem_limit_bytes=32 << 20),
        name="final",
    )(got.reshape(epochs, parts, 32 + height, side))


def solution(mesh):
    placed = (
        P(("epoch", "patch"), None, None),
        P(("epoch", "patch"), None, None),
        P(("epoch", "patch"), None),
        P(("epoch", "patch"), None),
        P(("epoch", "patch"), None),
        P(("epoch", "patch")),
        P(),
    )
    return jax.shard_map(
        shards,
        mesh=mesh,
        in_specs=placed,
        out_specs=(P("patch", "epoch", None), P("patch", "epoch", None)),
        check_vma=False,
    )
```

```python
import functools

import jax
import jax.numpy as jnp
import numpy as np
from jax import lax
from jax.experimental import pallas as pl
from jax.experimental.pallas import tpu as pltpu
from jax.sharding import PartitionSpec as P

SIGMAS = (1.0, 2.0, 3.5)
REACH = 7
GROUP = 4
WEIGHT_GROUP = 8
FIRST = 12
EARLY = (0,)


def blur_kernels(side):
    place = np.arange(side)
    distance = (place[:, None] - place[None, :]).astype(np.float32)
    taps = np.arange(-REACH, REACH + 1).astype(np.float32)
    tables = []
    for sigma in SIGMAS:
        scale = np.float32(2.0 * sigma * sigma)
        profile = np.where(np.abs(distance) <= REACH, np.exp(-distance * distance / scale), np.float32(0.0))
        tables.append(profile / np.sum(np.exp(-taps * taps / scale), dtype=np.float32))
    return np.concatenate(tables, axis=1).astype(jnp.bfloat16)


def keep_turned(value, off_c, wide_ref, first_row):
    rows, side = value.shape
    turned = pltpu.roll(value, off_c & (side - 1), 1)
    for h in range(2):
        lanes = turned[:, h * (side // 2) : (h + 1) * (side // 2)]
        wide_ref[h, first_row : first_row + rows] = lanes
        wide_ref[h, first_row + side : first_row + side + rows] = lanes


def table_of_tiles(patch_ref, off_ref, shape):
    lane = lax.broadcasted_iota(jnp.int32, shape, 1)
    row = lax.broadcasted_iota(jnp.int32, shape, 0)
    known = jnp.zeros(shape, jnp.int32)
    for t in range(patch_ref.shape[1]):
        mine = jnp.where(row == 0, patch_ref[0, t], jnp.where(row == 1, off_ref[0, t], off_ref[1, t]))
        known = jnp.where((lane == t) & (row < 3), mine, known)
    return known.astype(jnp.float32).astype(jnp.bfloat16)


def weight_body(patch_ref, off_ref, var_ref, out_ref, wide_ref):
    parts, group, height, side = out_ref.shape
    step = pl.program_id(0)
    half, swap = side // 2, height // 2
    chunk = 32

    @pl.when(step < pl.num_programs(0) - 1)
    def _():
        first = lax.broadcasted_iota(jnp.int32, (height, half), 0) < swap
        for t in range(group):
            tile = step * group + t
            off_r, off_c = off_ref[0, tile], off_ref[1, tile]
            for c in range(side // chunk):
                weight = 1.0 / var_ref[t, c * chunk : (c + 1) * chunk].astype(jnp.float32)
                keep_turned(weight, off_c, wide_ref.at[t], c * chunk)
            for part in range(parts):
                begins = [(4 * part - off_r) & (side - 1), (half + 4 * part - swap - off_r) & (side - 1)]
                for h in range(2):
                    rows = [wide_ref[t, h, pl.ds(begin, height)] for begin in begins]
                    out_ref[part, t, :, h * half : (h + 1) * half] = jnp.where(first, *rows).astype(jnp.bfloat16)

    @pl.when(step == pl.num_programs(0) - 1)
    def _():
        known = table_of_tiles(patch_ref, off_ref, (height, side))
        for part in range(parts):
            out_ref[part, 0] = known


def value_body(begin, tables, z_ref, core_ref, patch_ref, off_ref, visit_ref, scale_ref, coef_ref, kernel_ref, image_ref, var_ref, *refs):
    outs, (blur_ref, wide_ref) = refs[:8], refs[8:]
    group, height, side = outs[0].shape
    step = pl.program_id(0)
    half, band = side // 2, height // 2
    chunk = 32

    @pl.when(step < pl.num_programs(0) - tables)
    def _():
        lane = lax.broadcasted_iota(jnp.int32, (chunk, half), 1)
        row = lax.broadcasted_iota(jnp.int32, (chunk, half), 0)
        xs = [(2.0 * (lane + h * half).astype(jnp.float32) + 1.0) / side - 1.0 for h in range(2)]
        for t in range(group):
            tile = begin + step * group + t
            off_r, off_c = off_ref[0, tile], off_ref[1, tile]
            gain = scale_ref[visit_ref[tile]]
            k = [[coef_ref[6 * b + j, tile] for j in range(6)] for b in range(3)]
            square = [[k[b][5] * x for x in xs] for b in range(3)]
            row_pass = jnp.dot(image_ref[t], kernel_ref[...], preferred_element_type=jnp.float32).astype(jnp.bfloat16)
            for b in range(3):
                cols = slice(b * side, (b + 1) * side)
                blur_ref[t, b] = jnp.dot(kernel_ref[:, cols], row_pass[:, cols], preferred_element_type=jnp.float32)
            for c in range(side // chunk):
                rows = slice(c * chunk, (c + 1) * chunk)
                y = (2.0 * (row + c * chunk).astype(jnp.float32) + 1.0) / side - 1.0
                level = [k[b][0] + y * (k[b][1] + k[b][3] * y) for b in range(3)]
                slope = [k[b][2] + k[b][4] * y for b in range(3)]
                both = []
                for h in range(2):
                    cols = slice(h * half, (h + 1) * half)
                    matched = None
                    for b in range(3):
                        spatial = level[b] + xs[h] * (slope[b] + square[b][h])
                        term = spatial * blur_ref[t, b, rows, cols]
                        matched = term if matched is None else matched + term
                    both.append(gain * (1.0 / var_ref[t, rows, cols].astype(jnp.float32)) * matched)
                keep_turned(jnp.concatenate(both, axis=1), off_c, wide_ref.at[t], c * chunk)
            for m in range(8):
                member = (((z_ref[0] + (m & 3)) & 3) << 1) + (core_ref[0] ^ (m >> 2))
                for part in range(2):
                    top = (part * half + (member << 4) - off_r) & (side - 1)
                    for h in range(2):
                        rows = wide_ref[t, h, pl.ds(top, band)]
                        outs[m][t, part * band : (part + 1) * band, h * half : (h + 1) * half] = rows.astype(jnp.bfloat16)

    if tables:

        @pl.when(step == pl.num_programs(0) - 1)
        def _():
            known = table_of_tiles(patch_ref, off_ref, (height, side))
            for m in range(8):
                outs[m][0] = known


def clear_sums(sums_ref):
    zero = jnp.zeros(sums_ref.shape[1:], jnp.float32)

    def clear(p, unused):
        sums_ref[p] = zero
        return unused

    lax.fori_loop(0, sums_ref.shape[0], clear, 0)


def weight_sum_body(known_ref, part_ref, got_ref, out_ref, data_ref, sems, *sums_refs):
    sources, slots, height, side = got_ref.shape
    tiles, patches = slots - 1, out_ref.shape[1]
    bunch = sources // sems.shape[0]
    copies = [
        pltpu.make_async_copy(got_ref.at[pl.ds(n * bunch, bunch)], data_ref.at[pl.ds(n * bunch, bunch)], sems.at[n])
        for n in range(sems.shape[0])
    ]
    for copy in copies:
        copy.start()
    s = lax.broadcasted_iota(jnp.int32, (height, side), 0)
    row = (s >> 2) * (side // 2) + 4 * part_ref[0] + (s & 3)
    lane = lax.broadcasted_iota(jnp.int32, (height, side), 1)
    swap = height // 2
    first = s < swap
    for sums_ref in sums_refs:
        clear_sums(sums_ref)

    def add_source(source, unused):
        for t in range(tiles):
            p, off_r, off_c = known_ref[source, 0, t], known_ref[source, 1, t], known_ref[source, 2, t]
            sums_ref = sums_refs[t % len(sums_refs)]
            value = data_ref[source, t].astype(jnp.float32)
            left = jnp.where(lane >= off_c, value, 0.0)
            right = value - left
            upper = row >= off_r
            upper_left, upper_right = jnp.where(upper, left, 0.0), jnp.where(upper, right, 0.0)
            sums_ref[p, 0] += upper_left
            sums_ref[p, 1] += upper_right
            sums_ref[p, 2] += left - upper_left
            sums_ref[p, 3] += right - upper_right
        return unused

    for n, copy in enumerate(copies):
        copy.wait()
        lax.fori_loop(n * bunch, (n + 1) * bunch, add_source, 0)

    def one_patch(p, unused):
        for half in range(2):
            left, right = (sum(sums_ref[p, 2 * half + h] for sums_ref in sums_refs) for h in range(2))
            out_ref[2 * half, p] = jnp.where(first, left, pltpu.roll(right, swap, 0)).astype(jnp.bfloat16)
            out_ref[2 * half + 1, p] = jnp.where(first, pltpu.roll(left, swap, 0), right).astype(jnp.bfloat16)
        return unused

    lax.fori_loop(0, patches, one_patch, 0)


def add_values(known_ref, z_ref, core_ref, shares, got, data_ref, sums_ref, sems):
    _, _, height, side = data_ref.shape
    band = height // 2
    copies = [
        pltpu.make_async_copy(rows.at[pl.ds(0, tiles)], data_ref.at[n, pl.ds(0, tiles)], sems.at[n])
        for n, (rows, (m, begin, tiles)) in enumerate(zip(got, shares))
    ]
    for copy in copies:
        copy.start()
    zero = jnp.zeros(sums_ref.shape[1:], jnp.float32)

    def clear(p, unused):
        sums_ref[p] = zero
        return unused

    lax.fori_loop(0, sums_ref.shape[0], clear, 0)
    s = lax.broadcasted_iota(jnp.int32, (band, side), 0) + (((z_ref[0] << 1) + core_ref[0]) << 4)
    lane = lax.broadcasted_iota(jnp.int32, (band, side), 1)

    for n, (m, begin, tiles) in enumerate(shares):
        copies[n].wait()

        def some_tiles(step, unused):
            for u in range(4):
                t = 4 * step + u
                p, off_r, off_c = (known_ref[m, k, begin + t] for k in range(3))
                for part in range(2):
                    value = data_ref[n, t, part * band : (part + 1) * band].astype(jnp.float32)
                    left = jnp.where(lane >= off_c, value, 0.0)
                    right = value - left
                    upper = s >= off_r - part * (side // 2)
                    upper_left, upper_right = jnp.where(upper, left, 0.0), jnp.where(upper, right, 0.0)
                    sums_ref[p, part, 0] += upper_left
                    sums_ref[p, part, 1] += upper_right
                    sums_ref[p, 2 + part, 0] += left - upper_left
                    sums_ref[p, 2 + part, 1] += right - upper_right
            return unused

        lax.fori_loop(0, tiles // 4, some_tiles, 0)


def first_values_body(shares, known_ref, z_ref, core_ref, *refs):
    got, (out_ref, data_ref, sems) = refs[: len(shares)], refs[len(shares) :]
    add_values(known_ref, z_ref, core_ref, shares, got, data_ref, out_ref, sems)


def last_values_body(shares, known_ref, z_ref, core_ref, weight_ref, before_ref, middle_ref, *refs):
    got, (out_ref, data_ref, first_ref, second_ref, sums_ref, sems, before_sems) = refs[: len(shares)], refs[len(shares) :]
    band = sums_ref.shape[3]
    earlier = [
        pltpu.make_async_copy(before_ref, first_ref, before_sems.at[0]),
        pltpu.make_async_copy(middle_ref, second_ref, before_sems.at[1]),
    ]
    for copy in earlier:
        copy.start()
    add_values(known_ref, z_ref, core_ref, shares, got, data_ref, sums_ref, sems)
    for copy in earlier:
        copy.wait()

    def one_patch(p, unused):
        for quarter in range(4):
            for h in range(2):
                both = sums_ref[p, quarter, h] + first_ref[p, quarter, h] + second_ref[p, quarter, h]
                out_ref[quarter, p, h * band : (h + 1) * band] = both.astype(jnp.bfloat16)
            out_ref[quarter, p, 2 * band :] = weight_ref[quarter, p]
        return unused

    lax.fori_loop(0, out_ref.shape[1], one_patch, 0)


def final_body(got_ref, value_ref, weight_ref):
    epochs, parts, height, side = got_ref.shape
    band = 16
    for z in range(epochs):
        for core in range(2):
            rows = slice((2 * z + core) * band, (2 * z + core + 1) * band)
            for h in range(2):
                total = jnp.zeros((band, side), jnp.float32)
                for chip in range(parts // 2):
                    total += got_ref[z, 2 * chip + core, h * band : (h + 1) * band].astype(jnp.float32)
                value_ref[0, rows, h * side : (h + 1) * side] = total
    swap = 4
    first = lax.broadcasted_iota(jnp.int32, (8, side), 0) < swap
    for pair in range(parts // 2):
        both = []
        for part in (2 * pair, 2 * pair + 1):
            total = got_ref[0, part, 2 * band :].astype(jnp.float32)
            for e in range(1, epochs):
                total += got_ref[e, part, 2 * band :].astype(jnp.float32)
            both.append(total)
        rows = slice(pair * 8, (pair + 1) * 8)
        weight_ref[0, rows, :side] = jnp.where(first, both[0], pltpu.roll(both[1], swap, 0))
        weight_ref[0, rows, side:] = jnp.where(first, pltpu.roll(both[0], swap, 0), both[1])


def shards(tile_image, tile_var, psf_coef, tile_patch, tile_offset, tile_visit, visit_scale):
    count, side = tile_image.shape[:2]
    parts = lax.axis_size("patch")
    epochs = lax.axis_size("epoch")
    height = side // parts
    slots = count + 1
    z, j = lax.axis_index("epoch"), lax.axis_index("patch")
    place = [jnp.reshape(n, (1,)).astype(jnp.int32) for n in (z, j & 1, j)]
    table = jnp.asarray(blur_kernels(side))

    smem = pl.BlockSpec(memory_space=pltpu.SMEM)
    vmem = pl.BlockSpec(memory_space=pltpu.VMEM)
    steps = count // WEIGHT_GROUP
    tiles = pl.BlockSpec((WEIGHT_GROUP, side, side), lambda g: (jnp.minimum(g, steps - 1), 0, 0))
    pixels = count * side * side
    weights = pl.pallas_call(
        weight_body,
        grid=(steps + 1,),
        in_specs=[smem, smem, tiles],
        out_specs=pl.BlockSpec((parts, WEIGHT_GROUP, height, side), lambda g: (0, g, 0, 0)),
        out_shape=jax.ShapeDtypeStruct((parts, slots, height, side), jnp.bfloat16),
        scratch_shapes=[pltpu.VMEM((WEIGHT_GROUP, 2, 2 * side, side // 2), jnp.float32)],
        cost_estimate=pl.CostEstimate(flops=20 * pixels, bytes_accessed=4 * pixels, transcendentals=0),
        compiler_params=pltpu.CompilerParams(vmem_limit_bytes=60 << 20),
        name="weights",
    )(tile_patch.T, tile_offset.T, tile_var)
    def some_values(begin, end, tables, image):
        steps, group = (end - begin) // GROUP, begin // GROUP
        taken = pl.BlockSpec((GROUP, side, side), lambda g: (group + jnp.minimum(g, steps - 1), 0, 0))
        return pl.pallas_call(
            functools.partial(value_body, begin, tables),
            grid=(steps + tables,),
            in_specs=[smem] * 7 + [pl.BlockSpec((side, 3 * side), lambda g: (0, 0)), taken, taken],
            out_specs=[pl.BlockSpec((GROUP, 32, side), lambda g: (g, 0, 0))] * 8,
            out_shape=[jax.ShapeDtypeStruct((end - begin + tables, 32, side), jnp.bfloat16)] * 8,
            scratch_shapes=[
                pltpu.VMEM((GROUP, 3, side, side), jnp.float32),
                pltpu.VMEM((GROUP, 2, 2 * side, side // 2), jnp.float32),
            ],
            cost_estimate=pl.CostEstimate(flops=6 * pixels * side, bytes_accessed=3 * pixels, transcendentals=0),
            compiler_params=pltpu.CompilerParams(vmem_limit_bytes=60 << 20),
            name="values",
        )(*place[:2], tile_patch.T, tile_offset.T, tile_visit, visit_scale, psf_coef.T, table, image, tile_var)

    def share(m, rows):
        turn, other = m & 3, m >> 2
        pairs = [
            (e * parts + d, ((e + turn) % epochs) * parts + (d ^ other)) for e in range(epochs) for d in range(parts)
        ]
        return lax.ppermute(rows, ("epoch", "patch"), pairs)

    ints = lambda rows: rows.astype(jnp.float32).astype(jnp.int32)
    hbm = pl.BlockSpec(memory_space=pl.ANY)
    mine = jax.ShapeDtypeStruct((parts, 4, 2, 16, side), jnp.float32)
    tile_image, weights = lax.optimization_barrier((tile_image, weights))
    got_weights = lax.all_to_all(weights, "patch", split_axis=0, concat_axis=0, tiled=True)

    early = some_values(0, FIRST, 1, tile_image)
    got = {0: early[0]}
    for m in (1, 3, 2, 7, 5, 6, 4):
        got[m] = share(m, early[m])
    got = [got[m] for m in range(8)]
    tile_image, early_0 = lax.optimization_barrier((tile_image, early[0]))
    late = some_values(FIRST, count, 0, tile_image)
    more = {0: late[0]}
    for m in (1, 3, 2, 7, 5, 6):
        more[m] = share(m, late[m])
    known = ints(jnp.stack([g[FIRST, :3, :count] for g in got]))
    shares = [(m, 0, FIRST) for m in range(8)] + [(m, FIRST, count - FIRST) for m in EARLY]
    more[1], got[0], late_4 = lax.optimization_barrier((more[1], got[0], late[4]))
    def some_sums(shares, rows):
        return pl.pallas_call(
            functools.partial(first_values_body, shares),
            in_specs=[smem] * 3 + [hbm] * len(shares),
            out_specs=vmem,
            out_shape=mine,
            scratch_shapes=[
                pltpu.VMEM((len(shares), count - FIRST, 32, side), jnp.bfloat16),
                pltpu.SemaphoreType.DMA((len(shares),)),
            ],
            cost_estimate=pl.CostEstimate(flops=5 * pixels, bytes_accessed=3 * pixels, transcendentals=0),
            compiler_params=pltpu.CompilerParams(vmem_limit_bytes=56 << 20),
            name="value_sums",
        )(known, *place[:2], *rows)

    value_sums = some_sums(shares, [*got, *[more[m] for m in EARLY]])

    late_4, value_sums = lax.optimization_barrier((late_4, value_sums))
    more[4] = share(4, late_4)
    got_weights, value_sums = lax.optimization_barrier((got_weights, value_sums))
    weight_sums = pl.pallas_call(
        weight_sum_body,
        in_specs=[smem, smem, hbm],
        out_specs=vmem,
        out_shape=jax.ShapeDtypeStruct((4, parts, height, side), jnp.bfloat16),
        scratch_shapes=[
            pltpu.VMEM((parts, slots, height, side), jnp.bfloat16),
            pltpu.SemaphoreType.DMA((8,)),
            *[pltpu.VMEM((parts, 4, height, side), jnp.float32)] * 4,
        ],
        cost_estimate=pl.CostEstimate(flops=10 * pixels, bytes_accessed=3 * pixels, transcendentals=0),
        compiler_params=pltpu.CompilerParams(vmem_limit_bytes=60 << 20),
        name="weight_sums",
    )(ints(got_weights[:, count, :3, :count]), place[2], got_weights)
    middle = (1, 3, 2, 7, 5)
    later = {m: more[m] for m in middle}
    later[1], weight_sums = lax.optimization_barrier((later[1], weight_sums))
    middle_sums = some_sums([(m, FIRST, count - FIRST) for m in middle], [later[m] for m in middle])
    shares = [(m, FIRST, count - FIRST) for m in (4, 6)]
    sums = pl.pallas_call(
        functools.partial(last_values_body, shares),
        in_specs=[smem] * 3 + [vmem, hbm, hbm] + [hbm] * len(shares),
        out_specs=vmem,
        out_shape=jax.ShapeDtypeStruct((4, parts, 32 + height, side), jnp.bfloat16),
        scratch_shapes=[
            pltpu.VMEM((len(shares), count - FIRST, 32, side), jnp.bfloat16),
            *[pltpu.VMEM(mine.shape, jnp.float32)] * 3,
            pltpu.SemaphoreType.DMA((len(shares),)),
            pltpu.SemaphoreType.DMA((2,)),
        ],
        cost_estimate=pl.CostEstimate(flops=5 * pixels, bytes_accessed=3 * pixels, transcendentals=0),
        compiler_params=pltpu.CompilerParams(vmem_limit_bytes=56 << 20),
        name="last_value_sums",
    )(known, *place[:2], weight_sums, value_sums, middle_sums, *[more[m] for m, _, _ in shares])

    sums = sums.reshape(epochs * parts, 32 + height, side)
    got = lax.all_to_all(sums, ("epoch", "patch"), split_axis=0, concat_axis=0, tiled=True)
    quarter = jax.ShapeDtypeStruct((1, 4 * parts, 2 * side), jnp.float32)
    return pl.pallas_call(
        final_body,
        in_specs=[vmem],
        out_specs=(vmem, vmem),
        out_shape=(quarter, quarter),
        compiler_params=pltpu.CompilerParams(vmem_limit_bytes=32 << 20),
        name="final",
    )(got.reshape(epochs, parts, 32 + height, side))


def solution(mesh):
    placed = (
        P(("epoch", "patch"), None, None),
        P(("epoch", "patch"), None, None),
        P(("epoch", "patch"), None),
        P(("epoch", "patch"), None),
        P(("epoch", "patch"), None),
        P(("epoch", "patch")),
        P(),
    )
    return jax.shard_map(
        shards,
        mesh=mesh,
        in_specs=placed,
        out_specs=(P("patch", "epoch", None), P("patch", "epoch", None)),
        check_vma=False,
    )
```

```python
import functools

import jax
import jax.numpy as jnp
import numpy as np
from jax import lax
from jax.experimental import pallas as pl
from jax.experimental.pallas import tpu as pltpu
from jax.sharding import PartitionSpec as P

SIGMAS = (1.0, 2.0, 3.5)
REACH = 7
GROUP = 4
WEIGHT_GROUP = 8
FIRST = 12
EARLY = (0, 1, 3)


def blur_kernels(side):
    place = np.arange(side)
    distance = (place[:, None] - place[None, :]).astype(np.float32)
    taps = np.arange(-REACH, REACH + 1).astype(np.float32)
    tables = []
    for sigma in SIGMAS:
        scale = np.float32(2.0 * sigma * sigma)
        profile = np.where(np.abs(distance) <= REACH, np.exp(-distance * distance / scale), np.float32(0.0))
        tables.append(profile / np.sum(np.exp(-taps * taps / scale), dtype=np.float32))
    return np.concatenate(tables, axis=1).astype(jnp.bfloat16)


def keep_turned(value, off_c, wide_ref, first_row):
    rows, side = value.shape
    turned = pltpu.roll(value, off_c & (side - 1), 1)
    for h in range(2):
        lanes = turned[:, h * (side // 2) : (h + 1) * (side // 2)]
        wide_ref[h, first_row : first_row + rows] = lanes
        wide_ref[h, first_row + side : first_row + side + rows] = lanes


def table_of_tiles(patch_ref, off_ref, shape):
    lane = lax.broadcasted_iota(jnp.int32, shape, 1)
    row = lax.broadcasted_iota(jnp.int32, shape, 0)
    known = jnp.zeros(shape, jnp.int32)
    for t in range(patch_ref.shape[1]):
        mine = jnp.where(row == 0, patch_ref[0, t], jnp.where(row == 1, off_ref[0, t], off_ref[1, t]))
        known = jnp.where((lane == t) & (row < 3), mine, known)
    return known.astype(jnp.float32).astype(jnp.bfloat16)


def weight_body(patch_ref, off_ref, var_ref, out_ref, wide_ref):
    parts, group, height, side = out_ref.shape
    step = pl.program_id(0)
    half, swap = side // 2, height // 2
    chunk = 32

    @pl.when(step < pl.num_programs(0) - 1)
    def _():
        first = lax.broadcasted_iota(jnp.int32, (height, half), 0) < swap
        for t in range(group):
            tile = step * group + t
            off_r, off_c = off_ref[0, tile], off_ref[1, tile]
            for c in range(side // chunk):
                weight = 1.0 / var_ref[t, c * chunk : (c + 1) * chunk].astype(jnp.float32)
                keep_turned(weight, off_c, wide_ref.at[t], c * chunk)
            for part in range(parts):
                begins = [(4 * part - off_r) & (side - 1), (half + 4 * part - swap - off_r) & (side - 1)]
                for h in range(2):
                    rows = [wide_ref[t, h, pl.ds(begin, height)] for begin in begins]
                    out_ref[part, t, :, h * half : (h + 1) * half] = jnp.where(first, *rows).astype(jnp.bfloat16)

    @pl.when(step == pl.num_programs(0) - 1)
    def _():
        known = table_of_tiles(patch_ref, off_ref, (height, side))
        for part in range(parts):
            out_ref[part, 0] = known


def value_body(begin, tables, z_ref, core_ref, patch_ref, off_ref, visit_ref, scale_ref, coef_ref, kernel_ref, image_ref, var_ref, *refs):
    outs, (blur_ref, wide_ref) = refs[:8], refs[8:]
    group, height, side = outs[0].shape
    step = pl.program_id(0)
    half, band = side // 2, height // 2
    chunk = 32

    @pl.when(step < pl.num_programs(0) - tables)
    def _():
        lane = lax.broadcasted_iota(jnp.int32, (chunk, half), 1)
        row = lax.broadcasted_iota(jnp.int32, (chunk, half), 0)
        xs = [(2.0 * (lane + h * half).astype(jnp.float32) + 1.0) / side - 1.0 for h in range(2)]
        for t in range(group):
            tile = begin + step * group + t
            off_r, off_c = off_ref[0, tile], off_ref[1, tile]
            gain = scale_ref[visit_ref[tile]]
            k = [[coef_ref[6 * b + j, tile] for j in range(6)] for b in range(3)]
            square = [[k[b][5] * x for x in xs] for b in range(3)]
            row_pass = jnp.dot(image_ref[t], kernel_ref[...], preferred_element_type=jnp.float32).astype(jnp.bfloat16)
            for b in range(3):
                cols = slice(b * side, (b + 1) * side)
                blur_ref[t, b] = jnp.dot(kernel_ref[:, cols], row_pass[:, cols], preferred_element_type=jnp.float32)
            for c in range(side // chunk):
                rows = slice(c * chunk, (c + 1) * chunk)
                y = (2.0 * (row + c * chunk).astype(jnp.float32) + 1.0) / side - 1.0
                level = [k[b][0] + y * (k[b][1] + k[b][3] * y) for b in range(3)]
                slope = [k[b][2] + k[b][4] * y for b in range(3)]
                both = []
                for h in range(2):
                    cols = slice(h * half, (h + 1) * half)
                    matched = None
                    for b in range(3):
                        spatial = level[b] + xs[h] * (slope[b] + square[b][h])
                        term = spatial * blur_ref[t, b, rows, cols]
                        matched = term if matched is None else matched + term
                    both.append(gain * (1.0 / var_ref[t, rows, cols].astype(jnp.float32)) * matched)
                keep_turned(jnp.concatenate(both, axis=1), off_c, wide_ref.at[t], c * chunk)
            for m in range(8):
                member = (((z_ref[0] + (m & 3)) & 3) << 1) + (core_ref[0] ^ (m >> 2))
                for part in range(2):
                    top = (part * half + (member << 4) - off_r) & (side - 1)
                    for h in range(2):
                        rows = wide_ref[t, h, pl.ds(top, band)]
                        outs[m][t, part * band : (part + 1) * band, h * half : (h + 1) * half] = rows.astype(jnp.bfloat16)

    if tables:

        @pl.when(step == pl.num_programs(0) - 1)
        def _():
            known = table_of_tiles(patch_ref, off_ref, (height, side))
            for m in range(8):
                outs[m][0] = known


def clear_sums(sums_ref):
    zero = jnp.zeros(sums_ref.shape[1:], jnp.float32)

    def clear(p, unused):
        sums_ref[p] = zero
        return unused

    lax.fori_loop(0, sums_ref.shape[0], clear, 0)


def weight_sum_body(known_ref, part_ref, got_ref, out_ref, data_ref, sems, *sums_refs):
    sources, slots, height, side = got_ref.shape
    tiles, patches = slots - 1, out_ref.shape[1]
    bunch = sources // sems.shape[0]
    copies = [
        pltpu.make_async_copy(got_ref.at[pl.ds(n * bunch, bunch)], data_ref.at[pl.ds(n * bunch, bunch)], sems.at[n])
        for n in range(sems.shape[0])
    ]
    for copy in copies:
        copy.start()
    s = lax.broadcasted_iota(jnp.int32, (height, side), 0)
    row = (s >> 2) * (side // 2) + 4 * part_ref[0] + (s & 3)
    lane = lax.broadcasted_iota(jnp.int32, (height, side), 1)
    swap = height // 2
    first = s < swap
    for sums_ref in sums_refs:
        clear_sums(sums_ref)

    def add_source(source, unused):
        for t in range(tiles):
            p, off_r, off_c = known_ref[source, 0, t], known_ref[source, 1, t], known_ref[source, 2, t]
            sums_ref = sums_refs[t % len(sums_refs)]
            value = data_ref[source, t].astype(jnp.float32)
            left = jnp.where(lane >= off_c, value, 0.0)
            right = value - left
            upper = row >= off_r
            upper_left, upper_right = jnp.where(upper, left, 0.0), jnp.where(upper, right, 0.0)
            sums_ref[p, 0] += upper_left
            sums_ref[p, 1] += upper_right
            sums_ref[p, 2] += left - upper_left
            sums_ref[p, 3] += right - upper_right
        return unused

    for n, copy in enumerate(copies):
        copy.wait()
        lax.fori_loop(n * bunch, (n + 1) * bunch, add_source, 0)

    def one_patch(p, unused):
        for half in range(2):
            left, right = (sum(sums_ref[p, 2 * half + h] for sums_ref in sums_refs) for h in range(2))
            out_ref[2 * half, p] = jnp.where(first, left, pltpu.roll(right, swap, 0)).astype(jnp.bfloat16)
            out_ref[2 * half + 1, p] = jnp.where(first, pltpu.roll(left, swap, 0), right).astype(jnp.bfloat16)
        return unused

    lax.fori_loop(0, patches, one_patch, 0)


def add_values(known_ref, z_ref, core_ref, shares, got, data_ref, sums_ref, sems):
    _, _, height, side = data_ref.shape
    band = height // 2
    copies = [
        pltpu.make_async_copy(rows.at[pl.ds(0, tiles)], data_ref.at[n, pl.ds(0, tiles)], sems.at[n])
        for n, (rows, (m, begin, tiles)) in enumerate(zip(got, shares))
    ]
    for copy in copies:
        copy.start()
    zero = jnp.zeros(sums_ref.shape[1:], jnp.float32)

    def clear(p, unused):
        sums_ref[p] = zero
        return unused

    lax.fori_loop(0, sums_ref.shape[0], clear, 0)
    s = lax.broadcasted_iota(jnp.int32, (band, side), 0) + (((z_ref[0] << 1) + core_ref[0]) << 4)
    lane = lax.broadcasted_iota(jnp.int32, (band, side), 1)

    for n, (m, begin, tiles) in enumerate(shares):
        copies[n].wait()

        def some_tiles(step, unused):
            for u in range(4):
                t = 4 * step + u
                p, off_r, off_c = (known_ref[m, k, begin + t] for k in range(3))
                for part in range(2):
                    value = data_ref[n, t, part * band : (part + 1) * band].astype(jnp.float32)
                    left = jnp.where(lane >= off_c, value, 0.0)
                    right = value - left
                    upper = s >= off_r - part * (side // 2)
                    upper_left, upper_right = jnp.where(upper, left, 0.0), jnp.where(upper, right, 0.0)
                    sums_ref[p, part, 0] += upper_left
                    sums_ref[p, part, 1] += upper_right
                    sums_ref[p, 2 + part, 0] += left - upper_left
                    sums_ref[p, 2 + part, 1] += right - upper_right
            return unused

        lax.fori_loop(0, tiles // 4, some_tiles, 0)


def first_values_body(shares, known_ref, z_ref, core_ref, *refs):
    got, (out_ref, data_ref, sems) = refs[: len(shares)], refs[len(shares) :]
    add_values(known_ref, z_ref, core_ref, shares, got, data_ref, out_ref, sems)


def last_values_body(shares, known_ref, z_ref, core_ref, weight_ref, before_ref, *refs):
    got, (out_ref, data_ref, first_ref, sums_ref, sems, first_sem) = refs[: len(shares)], refs[len(shares) :]
    band = sums_ref.shape[3]
    earlier = pltpu.make_async_copy(before_ref, first_ref, first_sem)
    earlier.start()
    add_values(known_ref, z_ref, core_ref, shares, got, data_ref, sums_ref, sems)
    earlier.wait()

    def one_patch(p, unused):
        for quarter in range(4):
            for h in range(2):
                both = sums_ref[p, quarter, h] + first_ref[p, quarter, h]
                out_ref[quarter, p, h * band : (h + 1) * band] = both.astype(jnp.bfloat16)
            out_ref[quarter, p, 2 * band :] = weight_ref[quarter, p]
        return unused

    lax.fori_loop(0, out_ref.shape[1], one_patch, 0)


def final_body(got_ref, value_ref, weight_ref):
    epochs, parts, height, side = got_ref.shape
    band = 16
    for z in range(epochs):
        for core in range(2):
            rows = slice((2 * z + core) * band, (2 * z + core + 1) * band)
            for h in range(2):
                total = jnp.zeros((band, side), jnp.float32)
                for chip in range(parts // 2):
                    total += got_ref[z, 2 * chip + core, h * band : (h + 1) * band].astype(jnp.float32)
                value_ref[0, rows, h * side : (h + 1) * side] = total
    swap = 4
    first = lax.broadcasted_iota(jnp.int32, (8, side), 0) < swap
    for pair in range(parts // 2):
        both = []
        for part in (2 * pair, 2 * pair + 1):
            total = got_ref[0, part, 2 * band :].astype(jnp.float32)
            for e in range(1, epochs):
                total += got_ref[e, part, 2 * band :].astype(jnp.float32)
            both.append(total)
        rows = slice(pair * 8, (pair + 1) * 8)
        weight_ref[0, rows, :side] = jnp.where(first, both[0], pltpu.roll(both[1], swap, 0))
        weight_ref[0, rows, side:] = jnp.where(first, pltpu.roll(both[0], swap, 0), both[1])


def shards(tile_image, tile_var, psf_coef, tile_patch, tile_offset, tile_visit, visit_scale):
    count, side = tile_image.shape[:2]
    parts = lax.axis_size("patch")
    epochs = lax.axis_size("epoch")
    height = side // parts
    slots = count + 1
    z, j = lax.axis_index("epoch"), lax.axis_index("patch")
    place = [jnp.reshape(n, (1,)).astype(jnp.int32) for n in (z, j & 1, j)]
    table = jnp.asarray(blur_kernels(side))

    smem = pl.BlockSpec(memory_space=pltpu.SMEM)
    vmem = pl.BlockSpec(memory_space=pltpu.VMEM)
    steps = count // WEIGHT_GROUP
    tiles = pl.BlockSpec((WEIGHT_GROUP, side, side), lambda g: (jnp.minimum(g, steps - 1), 0, 0))
    pixels = count * side * side
    weights = pl.pallas_call(
        weight_body,
        grid=(steps + 1,),
        in_specs=[smem, smem, tiles],
        out_specs=pl.BlockSpec((parts, WEIGHT_GROUP, height, side), lambda g: (0, g, 0, 0)),
        out_shape=jax.ShapeDtypeStruct((parts, slots, height, side), jnp.bfloat16),
        scratch_shapes=[pltpu.VMEM((WEIGHT_GROUP, 2, 2 * side, side // 2), jnp.float32)],
        cost_estimate=pl.CostEstimate(flops=20 * pixels, bytes_accessed=4 * pixels, transcendentals=0),
        compiler_params=pltpu.CompilerParams(vmem_limit_bytes=60 << 20),
        name="weights",
    )(tile_patch.T, tile_offset.T, tile_var)
    def some_values(begin, end, tables, image):
        steps, group = (end - begin) // GROUP, begin // GROUP
        taken = pl.BlockSpec((GROUP, side, side), lambda g: (group + jnp.minimum(g, steps - 1), 0, 0))
        return pl.pallas_call(
            functools.partial(value_body, begin, tables),
            grid=(steps + tables,),
            in_specs=[smem] * 7 + [pl.BlockSpec((side, 3 * side), lambda g: (0, 0)), taken, taken],
            out_specs=[pl.BlockSpec((GROUP, 32, side), lambda g: (g, 0, 0))] * 8,
            out_shape=[jax.ShapeDtypeStruct((end - begin + tables, 32, side), jnp.bfloat16)] * 8,
            scratch_shapes=[
                pltpu.VMEM((GROUP, 3, side, side), jnp.float32),
                pltpu.VMEM((GROUP, 2, 2 * side, side // 2), jnp.float32),
            ],
            cost_estimate=pl.CostEstimate(flops=6 * pixels * side, bytes_accessed=3 * pixels, transcendentals=0),
            compiler_params=pltpu.CompilerParams(vmem_limit_bytes=60 << 20),
            name="values",
        )(*place[:2], tile_patch.T, tile_offset.T, tile_visit, visit_scale, psf_coef.T, table, image, tile_var)

    def share(m, rows):
        turn, other = m & 3, m >> 2
        pairs = [
            (e * parts + d, ((e + turn) % epochs) * parts + (d ^ other)) for e in range(epochs) for d in range(parts)
        ]
        return lax.ppermute(rows, ("epoch", "patch"), pairs)

    ints = lambda rows: rows.astype(jnp.float32).astype(jnp.int32)
    hbm = pl.BlockSpec(memory_space=pl.ANY)
    mine = jax.ShapeDtypeStruct((parts, 4, 2, 16, side), jnp.float32)
    tile_image, weights = lax.optimization_barrier((tile_image, weights))
    got_weights = lax.all_to_all(weights, "patch", split_axis=0, concat_axis=0, tiled=True)

    early = some_values(0, FIRST, 1, tile_image)
    got = {0: early[0]}
    for m in (1, 3, 2, 7, 5, 6, 4):
        got[m] = share(m, early[m])
    got = [got[m] for m in range(8)]
    tile_image, early_0 = lax.optimization_barrier((tile_image, early[0]))
    late = some_values(FIRST, count, 0, tile_image)
    more = {0: late[0]}
    for m in (1, 3, 2, 7, 5, 6):
        more[m] = share(m, late[m])
    known = ints(jnp.stack([g[FIRST, :3, :count] for g in got]))
    shares = [(m, 0, FIRST) for m in range(8)] + [(m, FIRST, count - FIRST) for m in EARLY]
    more[1], more[3], late_4 = lax.optimization_barrier((more[1], more[3], late[4]))
    value_sums = pl.pallas_call(
        functools.partial(first_values_body, shares),
        in_specs=[smem] * 3 + [hbm] * len(shares),
        out_specs=vmem,
        out_shape=mine,
        scratch_shapes=[
            pltpu.VMEM((len(shares), count - FIRST, 32, side), jnp.bfloat16),
            pltpu.SemaphoreType.DMA((len(shares),)),
        ],
        cost_estimate=pl.CostEstimate(flops=5 * pixels, bytes_accessed=3 * pixels, transcendentals=0),
        compiler_params=pltpu.CompilerParams(vmem_limit_bytes=56 << 20),
        name="first_value_sums",
    )(known, *place[:2], *got, *[more[m] for m in EARLY])

    late_4, value_sums = lax.optimization_barrier((late_4, value_sums))
    more[4] = share(4, late_4)
    got_weights, value_sums = lax.optimization_barrier((got_weights, value_sums))
    weight_sums = pl.pallas_call(
        weight_sum_body,
        in_specs=[smem, smem, hbm],
        out_specs=vmem,
        out_shape=jax.ShapeDtypeStruct((4, parts, height, side), jnp.bfloat16),
        scratch_shapes=[
            pltpu.VMEM((parts, slots, height, side), jnp.bfloat16),
            pltpu.SemaphoreType.DMA((8,)),
            *[pltpu.VMEM((parts, 4, height, side), jnp.float32)] * 4,
        ],
        cost_estimate=pl.CostEstimate(flops=10 * pixels, bytes_accessed=3 * pixels, transcendentals=0),
        compiler_params=pltpu.CompilerParams(vmem_limit_bytes=60 << 20),
        name="weight_sums",
    )(ints(got_weights[:, count, :3, :count]), place[2], got_weights)
    shares = [(m, FIRST, count - FIRST) for m in range(8) if m not in EARLY]
    sums = pl.pallas_call(
        functools.partial(last_values_body, shares),
        in_specs=[smem] * 3 + [vmem, hbm] + [hbm] * len(shares),
        out_specs=vmem,
        out_shape=jax.ShapeDtypeStruct((4, parts, 32 + height, side), jnp.bfloat16),
        scratch_shapes=[
            pltpu.VMEM((len(shares), count - FIRST, 32, side), jnp.bfloat16),
            pltpu.VMEM(mine.shape, jnp.float32),
            pltpu.VMEM(mine.shape, jnp.float32),
            pltpu.SemaphoreType.DMA((len(shares),)),
            pltpu.SemaphoreType.DMA,
        ],
        cost_estimate=pl.CostEstimate(flops=5 * pixels, bytes_accessed=3 * pixels, transcendentals=0),
        compiler_params=pltpu.CompilerParams(vmem_limit_bytes=56 << 20),
        name="last_value_sums",
    )(known, *place[:2], weight_sums, value_sums, *[more[m] for m, _, _ in shares])

    sums = sums.reshape(epochs * parts, 32 + height, side)
    got = lax.all_to_all(sums, ("epoch", "patch"), split_axis=0, concat_axis=0, tiled=True)
    quarter = jax.ShapeDtypeStruct((1, 4 * parts, 2 * side), jnp.float32)
    return pl.pallas_call(
        final_body,
        in_specs=[vmem],
        out_specs=(vmem, vmem),
        out_shape=(quarter, quarter),
        compiler_params=pltpu.CompilerParams(vmem_limit_bytes=32 << 20),
        name="final",
    )(got.reshape(epochs, parts, 32 + height, side))


def solution(mesh):
    placed = (
        P(("epoch", "patch"), None, None),
        P(("epoch", "patch"), None, None),
        P(("epoch", "patch"), None),
        P(("epoch", "patch"), None),
        P(("epoch", "patch"), None),
        P(("epoch", "patch")),
        P(),
    )
    return jax.shard_map(
        shards,
        mesh=mesh,
        in_specs=placed,
        out_specs=(P("patch", "epoch", None), P("patch", "epoch", None)),
        check_vma=False,
    )
```
